128 devices in a mesh: slab: 8 (over z, x_lo), view: 16 (over y, x_hi, core).
Axes of the slice: x: 4 (x_hi: 2, x_lo: 2; x = x_hi * 2 + x_lo), y: 4, z: 4, core: 2. Of those that a mesh axis runs over, the one named last changes fastest.
Arguments:
- volume: float32 [128, 32768], P(None, 'slab'), may hold values from 0 to 1
- measured: bfloat16 [32, 128, 2048], P('view'), may hold values from 0 to 8
- weights: bfloat16 [32, 32768, 1024], P('view', 'slab'), as said below
- offsets: int32 [32, 8], P('view', 'slab'), may hold values from 0 to 1024
- order: int32 [32], P('view'), may hold values from 0 to 1, as said below
Outputs:
- updated: float32 [128, 32768], P(None, 'slab')
- mismatch: float32 [32, 128, 2048], P('view')
The draws below stay inside these ranges and needn't reach their ends.
Inputs may be any that keep to these rules, and one draw needn't show every extreme that they name: `order`: each aligned group of 2 entries is a permutation of 0 to 1. `weights`: every weight is zero or positive, and every voxel has a positive weight in every view.
All inputs are finite; a program needn't handle non-finite values.
Results may differ from the reference program's by a relative error of at most 0.00055.
Values sent between devices are 32-bit elements; how exact they have to be, the bound alone decides.
A program may use at most 128 MiB of HBM per device.

```python
import math
import jax
import jax.numpy as jnp
from jax import lax

Z = 128
U = 2048
BAND = 1024
VOX_DEV = 4096
SUBSETS = 2
VOX = 32768
VIEWS = 32
N_SLAB = 8
N_VIEW = 16


FOOTPRINT = 4.0


def draw_weights(key, part):
    first_key = jax.random.fold_in(jax.random.fold_in(key, 11), 0)
    fourth_key = jax.random.fold_in(jax.random.fold_in(key, 11), 3)
    base = jnp.exp(jax.random.uniform(first_key, (VIEWS, VOX, BAND), jnp.float32, math.log(0.5), math.log(4.0)))
    voxel_place = (jnp.arange(VOX, dtype=jnp.float32) % VOX_DEV + 0.5) * (BAND / VOX_DEV)
    jitter = jax.random.uniform(fourth_key, (VIEWS, VOX, 1), jnp.float32, -2.0, 2.0)
    centre = jnp.clip(voxel_place[None, :, None] + jitter, 0.0, BAND - 1.0)
    columns = jnp.arange(BAND, dtype=jnp.float32)[None, None, :] + 0.5
    tent = jnp.maximum(1.0 - jnp.abs(columns - centre) / FOOTPRINT, 0.0)
    base = base * tent
    return (base * (BAND / (VOX_DEV * FOOTPRINT))).astype(jnp.bfloat16)


def draw_order(key, part):
    keys = jax.random.split(jax.random.fold_in(key, 23), VIEWS // SUBSETS)
    rows = jax.vmap(lambda single: jax.random.permutation(single, SUBSETS))(keys)
    return rows.astype(jnp.int32).reshape(VIEWS)


def set_ends(result, key, low, top_value):
    place = [jax.random.randint(jax.random.fold_in(key, axis), (), 0, length) for axis, length in enumerate(result.shape)]
    longest = result.shape.index(max(result.shape))
    neighbour = place[:longest] + [(place[longest] + 1) % result.shape[longest]] + place[longest + 1:]
    return result.at[tuple(place)].set(low).at[tuple(neighbour)].set(top_value)


def block_scale(key, extent, cuts, smallest, top_value):
    factor_of = 1.0
    for axis_at, blocks in cuts:
        draws = jax.random.uniform(jax.random.fold_in(jax.random.fold_in(key, 6), axis_at), (blocks,), jnp.float32, smallest / len(cuts), top_value / len(cuts))
        factor_of = factor_of * jnp.repeat(jnp.exp(draws), extent[axis_at] // blocks).reshape((-1,) + (1,) * (len(extent) - 1 - axis_at))
    return factor_of


def setup_inputs(seed: int = 0) -> dict:
    seeds = jax.random.split(jax.random.key(seed), 6)
    volume = jnp.clip(1.0 * jax.random.uniform(seeds[0], (Z, VOX), jnp.float32) ** block_scale(seeds[0], (Z, VOX), ((1, 8),), -0.2, 0.2), 0.0, 1.0)
    measured = jnp.clip(8.0 * jax.random.uniform(seeds[1], (VIEWS, Z, U), jnp.float32) ** block_scale(seeds[1], (VIEWS, Z, U), ((0, 16),), -0.2, 0.2), 0.0, 8.0).astype(jnp.bfloat16)
    weights = draw_weights(jax.random.fold_in(seeds[5], 71), 0)
    offsets = set_ends(jax.random.randint(seeds[3], (VIEWS, N_SLAB), 0, U - BAND + 1), jax.random.fold_in(seeds[3], 1), 0, U - BAND).astype(jnp.int32)
    order = draw_order(jax.random.fold_in(seeds[5], 71), 0)
    return {"volume": volume, "measured": measured, "weights": weights, "offsets": offsets, "order": order}


RELAXATION = 0.9


def reference(volume, measured, weights, offsets, order):
    current = volume
    mismatch = jnp.zeros((VIEWS, Z, U), jnp.float32)
    for subset_index in range(SUBSETS):
        volume_bf = current.astype(jnp.bfloat16)

        def one_view(group):
            chosen = group * SUBSETS + order[group * SUBSETS + subset_index]
            footprint = lax.dynamic_index_in_dim(weights, chosen, 0, keepdims=False)
            projection = jnp.zeros((Z, U), jnp.float32)
            row_total = jnp.zeros((U,), jnp.float32)
            for slab_index in range(N_SLAB):
                block = footprint[slab_index * VOX_DEV:(slab_index + 1) * VOX_DEV]
                first_column = offsets[chosen, slab_index]
                partial_value = jnp.dot(volume_bf[:, slab_index * VOX_DEV:(slab_index + 1) * VOX_DEV], block, preferred_element_type=jnp.float32)
                projection = projection + lax.dynamic_update_slice(jnp.zeros((Z, U), jnp.float32), partial_value, (jnp.int32(0), first_column))
                row_total = row_total + lax.dynamic_update_slice(jnp.zeros((U,), jnp.float32), jnp.sum(block, axis=0, dtype=jnp.float32), (first_column,))
            correction = (measured[chosen].astype(jnp.float32) - projection) / jnp.maximum(row_total, 1.0)
            back_parts = []
            for slab_index in range(N_SLAB):
                block = footprint[slab_index * VOX_DEV:(slab_index + 1) * VOX_DEV]
                band_values = lax.dynamic_slice_in_dim(correction, offsets[chosen, slab_index], BAND, 1).astype(jnp.bfloat16)
                back_parts.append(lax.dot_general(band_values, block, (((1,), (1,)), ((), ())), preferred_element_type=jnp.float32))
            back_terms = jnp.concatenate(back_parts, axis=1)
            col_total = jnp.sum(footprint, axis=1, dtype=jnp.float32)
            return back_terms, col_total, correction, chosen

        def accumulate(carry, group):
            back_terms, col_total, correction, chosen = one_view(group)
            return (carry[0] + back_terms, carry[1] + col_total), (correction, chosen)

        start_carry = (jnp.zeros((Z, VOX), jnp.float32), jnp.zeros((VOX,), jnp.float32))
        totals, outputs = lax.scan(accumulate, start_carry, jnp.arange(N_VIEW, dtype=jnp.int32))
        mismatch = mismatch.at[outputs[1]].set(outputs[0])
        current = current + RELAXATION * totals[0] / totals[1][None, :]
    return current, mismatch
```

```python
import jax
import jax.numpy as jnp
from jax import lax
from jax.experimental import pallas as pl
from jax.experimental.pallas import tpu as pltpu
from jax.sharding import PartitionSpec as P

RELAXATION = 0.9
MESH = pl.DeviceIdType.MESH
CHUNKS = 2
LANES = 128
KB = 512


def kernel(chunks, order_ref, off_ref, vol_hbm, meas_hbm, w_hbm, upd_hbm, mis_hbm,
           wv, vol, meas, acc, bandb, x1, xo, fs, fr, gs, gr, cor, rsum, csum,
           bk, rc, ry1, ry2, rx, local_sem, send_sem, recv_sem):
    slices, voxels = vol.shape
    rows = slices // chunks
    band = wv.shape[2]
    subsets = 2
    half = voxels // 2 // LANES
    nb = band // LANES

    s = lax.axis_index("slab")
    v = lax.axis_index("view")
    core = lax.rem(v, 2)
    xh = lax.rem(v // 2, 2)
    y = v // 4
    xl = lax.rem(s, 2)
    z = s // 2

    def slab_dev(other):
        return {"slab": other, "view": v}

    def view_dev(other):
        return {"slab": s, "view": other}

    y1 = y + 1 - 2 * lax.rem(y, 2)
    y3 = 3 - y
    y2 = lax.rem(y + 2, 4)
    dev_core = view_dev(v + 1 - 2 * core)
    dev_xh = view_dev(v + 2 - 4 * xh)
    dev_y1 = view_dev(v + 4 * (y1 - y))
    dev_y3 = view_dev(v + 4 * (y3 - y))
    s_mate = s + 1 - 2 * xl
    dev_mate = slab_dev(s_mate)
    dev_z = [None] + [slab_dev(lax.rem(z + k, 4) * 2 + xl) for k in (1, 2, 3)]

    used = [0]
    pending = []

    def remote(src, dst, dev, arrives=None):
        at = used[0]
        used[0] += 1
        cp = pltpu.make_async_remote_copy(
            src_ref=src, dst_ref=dst, send_sem=send_sem.at[at], recv_sem=recv_sem.at[at],
            device_id=dev, device_id_type=MESH)
        cp.start()
        pending.append(cp)
        if arrives is None:
            return cp
        return pltpu.make_async_remote_copy(
            src_ref=src, dst_ref=arrives, send_sem=send_sem.at[at], recv_sem=recv_sem.at[at],
            device_id=dev, device_id_type=MESH)

    steps = voxels // KB
    def w_copy(i):
        at = pl.ds(i * KB, KB)
        return pltpu.make_async_copy(w_hbm.at[:, at, :], wv.at[:, at, :], local_sem.at[i])
    vol_copies = []
    for c in range(chunks):
        at = pl.ds(c * rows, rows)
        cp = pltpu.make_async_copy(vol_hbm.at[at, :], vol.at[at, :], local_sem.at[steps + c])
        cp.start()
        vol_copies.append(cp)
        if c == 0:
            for i in range(steps):
                w_copy(i).start()
    meas_copies = []
    for hi in range(2):
        col = pl.multiple_of(hi * band + s * LANES, LANES)
        cp = pltpu.make_async_copy(meas_hbm.at[:, :, pl.ds(col, LANES)], meas.at[hi],
                                   local_sem.at[steps + chunks + hi])
        cp.start()
        meas_copies.append(cp)

    barrier = pltpu.get_barrier_semaphore()
    for k in range(1, 8):
        pl.semaphore_signal(barrier, inc=1, device_id=slab_dev(lax.rem(s + k, 8)), device_id_type=MESH)
    for dev in (dev_core, dev_xh, dev_y1, dev_y3):
        pl.semaphore_signal(barrier, inc=1, device_id=dev, device_id_type=MESH)
    pl.semaphore_wait(barrier, 11)

    column = lax.broadcasted_iota(jnp.int32, (8, LANES), 1) + s * LANES
    column = column.astype(jnp.float32)

    out_copies = []

    def chain(c):
        at_rows = pl.ds(c * rows, rows)
        ext = 8 if c == 0 else 0
        m = rows + 2 * ext
        r = rows + ext
        rr = pl.ds(0, r)
        only = pl.ds(0, rows)
        for t in range(subsets):
            view_t = order_ref[t]
            off = off_ref[view_t]
            shift = jnp.where(off >= band, 0, off)
            if t == 0:
                vol_copies[c].wait()
                if c == 0:
                    for i in range(steps):
                        w_copy(i).wait()
            acc[pl.ds(0, m), :] = jnp.zeros((m, band), jnp.float32)

            def forward(i, carry):
                if t == 0:
                    xk = vol[at_rows, pl.ds(pl.multiple_of(i * KB, KB), KB)]
                else:
                    xk = jnp.concatenate(
                        [x1[c, i * (KB // LANES) + j] for j in range(KB // LANES)], axis=1)
                xk = xk.astype(jnp.bfloat16)
                if ext:
                    xk = jnp.concatenate([xk, jnp.ones((2 * ext, KB), jnp.bfloat16)], axis=0)
                wk = wv[view_t, pl.ds(pl.multiple_of(i * KB, KB), KB), :]
                acc[pl.ds(0, m), :] += jnp.dot(xk, wk, preferred_element_type=jnp.float32)
                return carry

            lax.fori_loop(0, steps, forward, 0)
            folded = pltpu.roll(acc[rr, :], shift, 1)
            if ext:
                tail = folded[rows:, :]
                kind = lax.broadcasted_iota(jnp.int32, tail.shape, 0)
                tail = jnp.where(kind < 4, tail, off.astype(jnp.float32))
            for b in range(nb):
                fs[t, c, b, only, :] = folded[:rows, b * LANES:(b + 1) * LANES]
                if ext:
                    fs[t, c, b, pl.ds(rows, ext), :] = tail[:, b * LANES:(b + 1) * LANES]
            arrivals = []
            for k in range(1, 8):
                peer = lax.rem(s + k, 8)
                arrivals.append(remote(fs.at[t, c, peer, rr], fr.at[t, c, k, rr], slab_dev(peer)))
            yield
            fr[t, c, 0, rr, :] = fs[t, c, s, rr, :]
            for cp in arrivals:
                cp.wait_recv()
            if t == 0 and c == 0:
                for cp in meas_copies:
                    cp.wait()
            low = jnp.zeros((rows, LANES), jnp.float32)
            high = jnp.zeros((rows, LANES), jnp.float32)
            masks = []
            for k in range(8):
                offs = fr[t, 0, k, pl.ds(rows + 4, 1), :]
                masks.append(column[0:1, :] >= offs)
            if ext:
                rlow = jnp.zeros((1, LANES), jnp.float32)
                rhigh = jnp.zeros((1, LANES), jnp.float32)
                for k in range(8):
                    part = fr[t, c, k, pl.ds(rows, 1), :]
                    rlow += jnp.where(masks[k], part, 0.0)
                    rhigh += jnp.where(masks[k], 0.0, part)
                rsum[t, 0] = jnp.broadcast_to(jnp.maximum(rlow, 1.0), (8, LANES))
                rsum[t, 1] = jnp.broadcast_to(jnp.maximum(rhigh, 1.0), (8, LANES))
            for k in range(8):
                part = fr[t, c, k, only, :]
                low += jnp.where(masks[k], part, 0.0)
                high += jnp.where(masks[k], 0.0, part)
            seen_low = meas[0, view_t, at_rows, :].astype(jnp.float32)
            seen_high = meas[1, view_t, at_rows, :].astype(jnp.float32)
            low = (seen_low - low) / rsum[t, 0, pl.ds(0, 1), :]
            high = (seen_high - high) / rsum[t, 1, pl.ds(0, 1), :]
            cor[t, c, 0] = low
            cor[t, c, 1] = high
            arrivals = []
            for k in range(8):
                piece = jnp.where(masks[k], low, high)
                if k == 0:
                    gr[t, c, s] = piece
                else:
                    gs[t, c, k] = piece
                    arrivals.append(remote(
                        gs.at[t, c, k], gr.at[t, c, s], slab_dev(lax.rem(s + 8 - k, 8)),
                        gr.at[t, c, lax.rem(s + k, 8)]))
            own = pltpu.make_async_copy(cor.at[t, c], mis_hbm.at[t, c, s],
                                        local_sem.at[steps + chunks + 2 + t * chunks + c])
            own.start()
            out_copies.append(own)
            mate_in = remote(cor.at[t, c], mis_hbm.at[t, c, s], dev_mate, mis_hbm.at[t, c, s_mate])
            for k in (1, 2, 3):
                far = lax.rem(z + 4 - k, 4) * 2 + xl
                out_copies.append(("recv", remote(
                    cor.at[t, c], mis_hbm.at[t, c, s], dev_z[k], mis_hbm.at[t, c, far])))
            yield
            for cp in arrivals:
                cp.wait_recv()
            g = jnp.concatenate([gr[t, c, b] for b in range(nb)], axis=1)
            g = pltpu.roll(g, jnp.where(shift == 0, 0, band - shift), 1).astype(jnp.bfloat16)
            bandb[only, :] = g
            if ext:
                bandb[pl.ds(rows, 2 * ext), :] = jnp.ones((2 * ext, band), jnp.bfloat16)

            def backward(base):
                def step(n, carry):
                    vb = base + n * (KB // LANES)
                    wk = wv[view_t, pl.ds(pl.multiple_of(vb * LANES, LANES), KB), :]
                    res = lax.dot_general(bandb[pl.ds(0, m), :], wk, (((1,), (1,)), ((), ())),
                                          preferred_element_type=jnp.float32)
                    for j in range(KB // LANES):
                        bk[t, c, vb + j, rr, :] = res[:r, j * LANES:(j + 1) * LANES]
                    return carry
                lax.fori_loop(0, half * LANES // KB, step, 0)

            theirs = (1 - core) * half
            mine = core * half
            backward(theirs)
            core_in = remote(bk.at[t, c, pl.ds(theirs, half), rr], rc.at[t, c, :, rr], dev_core)
            backward(mine)
            mate_in.wait_recv()
            for k in (1, 2, 3):
                far = lax.rem(z + 4 - k, 4) * 2 + 1 - xl
                out_copies.append(("recv", remote(
                    mis_hbm.at[t, c, s_mate], mis_hbm.at[t, c, s_mate], dev_z[k],
                    mis_hbm.at[t, c, far])))
            yield
            core_in.wait_recv()

            def add(block, extra, start):
                for j in range(2):
                    at = mine + block + j
                    bk[t, c, at, rr, :] += rc[t, c, block + j, rr, :]
                    if extra is not None:
                        bk[t, c, at, rr, :] += extra[j, rr, :]

            ins = []
            for h in range(2):
                to, first = ((dev_y1, y1), (dev_y3, y3))[h]
                for j, yb in enumerate((first, y2)):
                    block = h * 8 + yb * 2
                    add(block, None, None)
                    ins.append(remote(bk.at[t, c, pl.ds(mine + block, 2), rr],
                                      ry1.at[t, c, h, j, :, rr], to))
            yield
            for cp in ins:
                cp.wait_recv()
            ins = []
            for h in range(2):
                to, second = ((dev_y3, y3), (dev_y1, y1))[h]
                block = h * 8 + second * 2
                add(block, ry1.at[t, c, h, 1], None)
                ins.append(remote(bk.at[t, c, pl.ds(mine + block, 2), rr],
                                  ry2.at[t, c, h, :, rr], to))
            for h in range(2):
                add(h * 8 + y * 2, ry1.at[t, c, h, 0], None)
            yield
            for cp in ins:
                cp.wait_recv()
            ins = []
            for h in range(2):
                at = mine + h * 8 + y * 2
                bk[t, c, at + 1 - xh, rr, :] += ry2[t, c, h, 1 - xh, rr, :]
                ins.append(remote(bk.at[t, c, at + 1 - xh, rr], rx.at[t, c, h, rr], dev_xh))
                bk[t, c, at + xh, rr, :] += ry2[t, c, h, xh, rr, :]
            yield
            for cp in ins:
                cp.wait_recv()
            x_new = x1 if t == 0 else xo
            ins = []
            for h in range(2):
                vb = mine + h * 8 + y * 2 + xh
                total = bk[t, c, vb, rr, :] + rx[t, c, h, rr, :]
                if ext:
                    csum[t, h] = total[rows:, :]
                if t == 0:
                    old = vol[at_rows, pl.ds(pl.multiple_of(vb * LANES, LANES), LANES)]
                else:
                    old = x1[c, vb]
                x_new[c, vb] = old + RELAXATION * total[:rows, :] / csum[t, h, pl.ds(0, 1), :]
                ins.append(remote(x_new.at[c, vb], x_new.at[c, vb], dev_xh,
                                  x_new.at[c, vb + 1 - 2 * xh]))
            yield
            for cp in ins:
                cp.wait_recv()

            def blocks(h, yb):
                return x_new.at[c, pl.ds(mine + h * 8 + yb * 2, 2)]

            ins = []
            for h in range(2):
                to, got = ((dev_y3, y3), (dev_y1, y1))[h]
                ins.append(remote(blocks(h, y), blocks(h, y), to, blocks(h, got)))
            yield
            for cp in ins:
                cp.wait_recv()
            ins = []
            for h in range(2):
                to, held, got = ((dev_y1, y3, y1), (dev_y3, y1, y3))[h]
                ins.append(remote(blocks(h, y), blocks(h, y), to, blocks(h, got)))
                ins.append(remote(blocks(h, held), blocks(h, held), to, blocks(h, y2)))
            yield
            for cp in ins:
                cp.wait_recv()
            whole = x_new.at[c, pl.ds(mine, half)]
            core_in = remote(whole, whole, dev_core, x_new.at[c, pl.ds(theirs, half)])
            yield
            core_in.wait_recv()
        done = pltpu.make_async_copy(xo.at[c], upd_hbm.at[c],
                                     local_sem.at[steps + chunks + 2 + subsets * chunks + c])
        done.start()
        out_copies.append(done)

    live = [chain(c) for c in range(chunks)]
    while live:
        still = []
        for g in live:
            try:
                next(g)
                still.append(g)
            except StopIteration:
                pass
        live = still
    for cp in out_copies:
        if isinstance(cp, tuple):
            cp[1].wait_recv()
        else:
            cp.wait()
    for cp in pending:
        cp.wait_send()


def per_device(volume, measured, weights, offsets, order):
    subsets, voxels, band = weights.shape
    slices = volume.shape[0]
    cols = measured.shape[2]
    chunks = CHUNKS
    rows = slices // chunks
    r = rows + 8
    nb = band // LANES
    vb = voxels // LANES
    f32 = jnp.float32
    copies = 39 * subsets * chunks
    any_spec = pl.BlockSpec(memory_space=pl.ANY)
    smem = pl.BlockSpec(memory_space=pltpu.SMEM)
    upd, mis = pl.pallas_call(
        lambda *refs: kernel(chunks, *refs),
        out_shape=(jax.ShapeDtypeStruct((chunks, vb, rows, LANES), f32),
                   jax.ShapeDtypeStruct((subsets, chunks, nb, 2, rows, LANES), f32)),
        in_specs=[smem, smem, any_spec, any_spec, any_spec],
        out_specs=(any_spec, any_spec),
        scratch_shapes=[
            pltpu.VMEM((subsets, voxels, band), jnp.bfloat16),
            pltpu.VMEM((slices, voxels), f32),
            pltpu.VMEM((2, subsets, slices, LANES), jnp.bfloat16),
            pltpu.VMEM((rows + 16, band), f32),
            pltpu.VMEM((rows + 16, band), jnp.bfloat16),
            pltpu.VMEM((chunks, vb, rows, LANES), f32),
            pltpu.VMEM((chunks, vb, rows, LANES), f32),
            pltpu.VMEM((subsets, chunks, nb, r, LANES), f32),
            pltpu.VMEM((subsets, chunks, nb, r, LANES), f32),
            pltpu.VMEM((subsets, chunks, nb, rows, LANES), f32),
            pltpu.VMEM((subsets, chunks, nb, rows, LANES), f32),
            pltpu.VMEM((subsets, chunks, 2, rows, LANES), f32),
            pltpu.VMEM((subsets, 2, 8, LANES), f32),
            pltpu.VMEM((subsets, 2, 8, LANES), f32),
            pltpu.VMEM((subsets, chunks, vb, r, LANES), f32),
            pltpu.VMEM((subsets, chunks, vb // 2, r, LANES), f32),
            pltpu.VMEM((subsets, chunks, 2, 2, 2, r, LANES), f32),
            pltpu.VMEM((subsets, chunks, 2, 2, r, LANES), f32),
            pltpu.VMEM((subsets, chunks, 2, r, LANES), f32),
            pltpu.SemaphoreType.DMA((voxels // KB + chunks * 2 + 2 + subsets * chunks,)),
            pltpu.SemaphoreType.DMA((copies,)),
            pltpu.SemaphoreType.DMA((copies,)),
        ],
        compiler_params=pltpu.CompilerParams(
            collective_id=0, has_side_effects=True, vmem_limit_bytes=56 * 2**20),
        name="sart",
    )(order, offsets.reshape(subsets), volume, measured, weights)
    updated = jnp.transpose(upd, (0, 2, 1, 3)).reshape(slices, voxels)
    mis = jnp.where(order[0] == 0, mis, mis[::-1])
    mismatch = jnp.transpose(mis, (0, 1, 4, 3, 2, 5)).reshape(subsets, slices, cols)
    return updated, mismatch


def solution(mesh):
    placed = (
        P(None, "slab"),
        P("view", None, None),
        P("view", "slab", None),
        P("view", "slab"),
        P("view"),
    )
    return jax.shard_map(
        per_device,
        mesh=mesh,
        in_specs=placed,
        out_specs=(P(None, "slab"), P("view", None, None)),
        check_vma=False,
    )
```

```python
import jax
import jax.numpy as jnp
from jax import lax
from jax.experimental import pallas as pl
from jax.experimental.pallas import tpu as pltpu
from jax.sharding import PartitionSpec as P

RELAXATION = 0.9
MESH = pl.DeviceIdType.MESH
CHUNKS = 2
LANES = 128
KB = 1024
FAR_FIRST = ((2, 1), (1, 1), (3, 1), (0, 1), (2, 0), (1, 0), (3, 0))


def kernel(chunks, order_ref, off_ref, vol_hbm, meas_hbm, w_hbm, upd_hbm, mis_hbm,
           wv, vol, meas, acc, bandb, x1, xo, fs, fr, gs, gr, cor, rsum, csum,
           bk, rc, rv, obuf, local_sem, send_sem, recv_sem):
    slices, voxels = vol.shape
    rows = slices // chunks
    band = wv.shape[2]
    subsets = 2
    half = voxels // 2 // LANES
    nb = band // LANES

    s = lax.axis_index("slab")
    v = lax.axis_index("view")
    core = lax.rem(v, 2)
    xh = lax.rem(v // 2, 2)
    y = v // 4
    xl = lax.rem(s, 2)
    z = s // 2

    def slab_dev(other):
        return {"slab": other, "view": v}

    def view_dev(other):
        return {"slab": s, "view": other}

    dev_core = view_dev(v + 1 - 2 * core)

    def share(dy, dx):
        return lax.rem(y + dy, 4) * 2 + (1 - xh if dx else xh)

    s_mate = s + 1 - 2 * xl
    dev_mate = slab_dev(s_mate)
    dev_z = [None] + [slab_dev(lax.rem(z + k, 4) * 2 + xl) for k in (1, 2, 3)]

    used = [0]
    pending = []

    def remote(src, dst, dev, arrives=None):
        at = used[0]
        used[0] += 1
        cp = pltpu.make_async_remote_copy(
            src_ref=src, dst_ref=dst, send_sem=send_sem.at[at], recv_sem=recv_sem.at[at],
            device_id=dev, device_id_type=MESH)
        cp.start()
        pending.append(cp)
        if arrives is None:
            return cp
        return pltpu.make_async_remote_copy(
            src_ref=src, dst_ref=arrives, send_sem=send_sem.at[at], recv_sem=recv_sem.at[at],
            device_id=dev, device_id_type=MESH)

    steps = voxels // KB
    def w_copy(i):
        at = pl.ds(i * KB, KB)
        return pltpu.make_async_copy(w_hbm.at[:, at, :], wv.at[:, at, :], local_sem.at[i])
    vol_copies = []
    for c in range(chunks):
        at = pl.ds(c * rows, rows)
        cp = pltpu.make_async_copy(vol_hbm.at[at, :], vol.at[at, :], local_sem.at[steps + c])
        cp.start()
        vol_copies.append(cp)
        if c == 0:
            for i in range(steps):
                w_copy(i).start()
    meas_copies = []
    for hi in range(2):
        col = pl.multiple_of(hi * band + s * LANES, LANES)
        cp = pltpu.make_async_copy(meas_hbm.at[:, :, pl.ds(col, LANES)], meas.at[hi],
                                   local_sem.at[steps + chunks + hi])
        cp.start()
        meas_copies.append(cp)

    barrier = pltpu.get_barrier_semaphore()
    for k in range(1, 8):
        pl.semaphore_signal(barrier, inc=1, device_id=slab_dev(lax.rem(s + k, 8)), device_id_type=MESH)
    pl.semaphore_signal(barrier, inc=1, device_id=dev_core, device_id_type=MESH)
    for dy, dx in FAR_FIRST:
        pl.semaphore_signal(barrier, inc=1, device_id=view_dev(share(dy, dx) * 2 + core), device_id_type=MESH)

    column = lax.broadcasted_iota(jnp.int32, (8, LANES), 1) + s * LANES
    column = column.astype(jnp.float32)

    out_copies = []

    def chain(c):
        at_rows = pl.ds(c * rows, rows)
        ext = 8 if c == 0 else 0
        m = rows + 2 * ext
        r = rows + ext
        rr = pl.ds(0, r)
        only = pl.ds(0, rows)
        for t in range(subsets):
            view_t = order_ref[t]
            off = off_ref[view_t]
            shift = jnp.where(off >= band, 0, off)
            if t == 0:
                vol_copies[c].wait()
            acc[pl.ds(0, m), :] = jnp.zeros((m, band), jnp.float32)

            def forward(i, carry):
                at = pl.ds(pl.multiple_of(i * KB, KB), KB)
                if t == 0:
                    xk = vol[at_rows, at]
                else:
                    xk = jnp.concatenate(
                        [x1[c, i * (KB // LANES) + j] for j in range(KB // LANES)], axis=1)
                xk = xk.astype(jnp.bfloat16)
                if ext:
                    xk = jnp.concatenate([xk, jnp.ones((2 * ext, KB), jnp.bfloat16)], axis=0)
                if t == 0 and c == 0:
                    w_copy(i).wait()
                    wk = jnp.where(view_t == 0, wv[0, at, :], wv[1, at, :])
                else:
                    wk = wv[view_t, at, :]
                acc[pl.ds(0, m), :] += jnp.dot(xk, wk, preferred_element_type=jnp.float32)
                return carry

            if t == 0:
                lax.fori_loop(0, steps, forward, 0)
            else:
                lax.fori_loop(core * (steps // 2), (core + 1) * (steps // 2), forward, 0)
                core_in.wait_recv()
                lax.fori_loop((1 - core) * (steps // 2), (2 - core) * (steps // 2), forward, 0)
            if t == 0 and c == 0:
                pl.semaphore_wait(barrier, 15)
            folded = pltpu.roll(acc[rr, :], shift, 1)
            if ext:
                tail = folded[rows:, :]
                kind = lax.broadcasted_iota(jnp.int32, tail.shape, 0)
                tail = jnp.where(kind < 4, tail, off.astype(jnp.float32))
            for b in range(nb):
                fs[t, c, b, only, :] = folded[:rows, b * LANES:(b + 1) * LANES]
                if ext:
                    fs[t, c, b, pl.ds(rows, ext), :] = tail[:, b * LANES:(b + 1) * LANES]
            arrivals = []
            for k in range(1, 8):
                peer = lax.rem(s + k, 8)
                arrivals.append(remote(fs.at[t, c, peer, rr], fr.at[t, c, k, rr], slab_dev(peer)))
            yield
            fr[t, c, 0, rr, :] = fs[t, c, s, rr, :]
            for cp in arrivals:
                cp.wait_recv()
            if t == 0 and c == 0:
                for cp in meas_copies:
                    cp.wait()
            low = jnp.zeros((rows, LANES), jnp.float32)
            high = jnp.zeros((rows, LANES), jnp.float32)
            masks = []
            for k in range(8):
                offs = fr[t, 0, k, pl.ds(rows + 4, 1), :]
                masks.append(column[0:1, :] >= offs)
            if ext:
                rlow = jnp.zeros((1, LANES), jnp.float32)
                rhigh = jnp.zeros((1, LANES), jnp.float32)
                for k in range(8):
                    part = fr[t, c, k, pl.ds(rows, 1), :]
                    rlow += jnp.where(masks[k], part, 0.0)
                    rhigh += jnp.where(masks[k], 0.0, part)
                rsum[t, 0] = jnp.broadcast_to(jnp.maximum(rlow, 1.0), (8, LANES))
                rsum[t, 1] = jnp.broadcast_to(jnp.maximum(rhigh, 1.0), (8, LANES))
            for k in range(8):
                part = fr[t, c, k, only, :]
                low += jnp.where(masks[k], part, 0.0)
                high += jnp.where(masks[k], 0.0, part)
            seen_low = meas[0, view_t, at_rows, :].astype(jnp.float32)
            seen_high = meas[1, view_t, at_rows, :].astype(jnp.float32)
            low = (seen_low - low) / rsum[t, 0, pl.ds(0, 1), :]
            high = (seen_high - high) / rsum[t, 1, pl.ds(0, 1), :]
            cor[t, 0, at_rows, :] = low
            cor[t, 1, at_rows, :] = high
            arrivals = []
            for k in range(8):
                piece = jnp.where(masks[k], low, high)
                if k == 0:
                    gr[t, c, s] = piece
                else:
                    gs[t, c, k] = piece
                    arrivals.append(remote(
                        gs.at[t, c, k], gr.at[t, c, s], slab_dev(lax.rem(s + 8 - k, 8)),
                        gr.at[t, c, lax.rem(s + k, 8)]))
            if c == chunks - 1:
                def cols(slab):
                    at = pl.ds(pl.multiple_of(slab * LANES, LANES), LANES)
                    return mis_hbm.at[t, :, :, at]
                own = pltpu.make_async_copy(cor.at[t], cols(s), local_sem.at[steps + chunks + 2 + t])
                own.start()
                out_copies.append(own)
                mate_in = remote(cor.at[t], cols(s), dev_mate, cols(s_mate))
                for k in (1, 2, 3):
                    far = lax.rem(z + 4 - k, 4) * 2 + xl
                    out_copies.append(("recv", remote(cor.at[t], cols(s), dev_z[k], cols(far))))
            yield
            for cp in arrivals:
                cp.wait_recv()
            g = jnp.concatenate([gr[t, c, b] for b in range(nb)], axis=1)
            g = pltpu.roll(g, jnp.where(shift == 0, 0, band - shift), 1).astype(jnp.bfloat16)
            bandb[only, :] = g
            if ext:
                bandb[pl.ds(rows, 2 * ext), :] = jnp.ones((2 * ext, band), jnp.bfloat16)

            def backward(base):
                def step(n, carry):
                    vb = base + n * (KB // LANES)
                    wk = wv[view_t, pl.ds(pl.multiple_of(vb * LANES, LANES), KB), :]
                    res = lax.dot_general(bandb[pl.ds(0, m), :], wk, (((1,), (1,)), ((), ())),
                                          preferred_element_type=jnp.float32)
                    for j in range(KB // LANES):
                        bk[t, c, vb + j, rr, :] = res[:r, j * LANES:(j + 1) * LANES]
                    return carry
                lax.fori_loop(0, half * LANES // KB, step, 0)

            theirs = (1 - core) * half
            mine = core * half
            backward(theirs)
            core_in = remote(bk.at[t, c, pl.ds(theirs, half), rr], rc.at[t, c, :, rr], dev_core)
            backward(mine)
            if c == chunks - 1:
                mate_in.wait_recv()
                for k in (1, 2, 3):
                    far = lax.rem(z + 4 - k, 4) * 2 + 1 - xl
                    out_copies.append(("recv", remote(cols(s_mate), cols(s_mate), dev_z[k], cols(far))))
            yield
            core_in.wait_recv()

            def add(q):
                for j in range(2):
                    bk[t, c, mine + q * 2 + j, rr, :] += rc[t, c, q * 2 + j, rr, :]

            ins = []
            for k, (dy, dx) in enumerate(FAR_FIRST):
                q = share(dy, dx)
                add(q)
                ins.append(remote(bk.at[t, c, pl.ds(mine + q * 2, 2), rr], rv.at[t, c, k, :, rr],
                                  view_dev(q * 2 + core)))
            q = share(0, 0)
            add(q)
            yield
            for cp in ins:
                cp.wait_recv()
            x_new = x1 if t == 0 else xo
            for j in range(2):
                vb = mine + q * 2 + j
                total = bk[t, c, vb, rr, :]
                for k in range(7):
                    total += rv[t, c, k, j, rr, :]
                if ext:
                    csum[t, j] = total[rows:, :]
                if t == 0:
                    old = vol[at_rows, pl.ds(pl.multiple_of(vb * LANES, LANES), LANES)]
                else:
                    old = x1[c, vb]
                x_new[c, vb] = old + RELAXATION * total[:rows, :] / csum[t, j, pl.ds(0, 1), :]
            ins = []

            def piece(q):
                return x_new.at[c, pl.ds(mine + q * 2, 2)]

            for dy, dx in FAR_FIRST:
                to = share(dy, dx)
                ins.append(remote(piece(q), piece(q), view_dev(to * 2 + core), piece(share(4 - dy, dx))))
            yield
            for cp in ins:
                cp.wait_recv()
            whole = x_new.at[c, pl.ds(mine, half)]
            core_in = remote(whole, whole, dev_core, x_new.at[c, pl.ds(theirs, half)])
            yield

        def lay_out(base):
            for j in range(half):
                at = pl.ds(pl.multiple_of((base + j) * LANES, LANES), LANES)
                obuf[at_rows, at] = xo[c, base + j]

        lay_out(mine)
        core_in.wait_recv()
        lay_out(theirs)
        done = pltpu.make_async_copy(obuf.at[at_rows, :], upd_hbm.at[at_rows, :],
                                     local_sem.at[steps + chunks + 2 + subsets + c])
        done.start()
        out_copies.append(done)

    live = [chain(c) for c in range(chunks)]
    while live:
        still = []
        for g in live:
            try:
                next(g)
                still.append(g)
            except StopIteration:
                pass
        live = still
    for cp in out_copies:
        if isinstance(cp, tuple):
            cp[1].wait_recv()
        else:
            cp.wait()
    for cp in pending:
        cp.wait_send()


def per_device(volume, measured, weights, offsets, order):
    subsets, voxels, band = weights.shape
    slices = volume.shape[0]
    cols = measured.shape[2]
    chunks = CHUNKS
    rows = slices // chunks
    r = rows + 8
    nb = band // LANES
    vb = voxels // LANES
    f32 = jnp.float32
    copies = (7 * 4 + 2) * subsets * chunks + 7 * subsets
    any_spec = pl.BlockSpec(memory_space=pl.ANY)
    smem = pl.BlockSpec(memory_space=pltpu.SMEM)
    upd, mis = pl.pallas_call(
        lambda *refs: kernel(chunks, *refs),
        out_shape=(jax.ShapeDtypeStruct((slices, voxels), f32),
                   jax.ShapeDtypeStruct((subsets, 2, slices, band), f32)),
        in_specs=[smem, smem, any_spec, any_spec, any_spec],
        out_specs=(any_spec, any_spec),
        scratch_shapes=[
            pltpu.VMEM((subsets, voxels, band), jnp.bfloat16),
            pltpu.VMEM((slices, voxels), f32),
            pltpu.VMEM((2, subsets, slices, LANES), jnp.bfloat16),
            pltpu.VMEM((rows + 16, band), f32),
            pltpu.VMEM((rows + 16, band), jnp.bfloat16),
            pltpu.VMEM((chunks, vb, rows, LANES), f32),
            pltpu.VMEM((chunks, vb, rows, LANES), f32),
            pltpu.VMEM((subsets, chunks, nb, r, LANES), f32),
            pltpu.VMEM((subsets, chunks, nb, r, LANES), f32),
            pltpu.VMEM((subsets, chunks, nb, rows, LANES), f32),
            pltpu.VMEM((subsets, chunks, nb, rows, LANES), f32),
            pltpu.VMEM((subsets, 2, slices, LANES), f32),
            pltpu.VMEM((subsets, 2, 8, LANES), f32),
            pltpu.VMEM((subsets, 2, 8, LANES), f32),
            pltpu.VMEM((subsets, chunks, vb, r, LANES), f32),
            pltpu.VMEM((subsets, chunks, vb // 2, r, LANES), f32),
            pltpu.VMEM((subsets, chunks, 7, 2, r, LANES), f32),
            pltpu.VMEM((slices, voxels), f32),
            pltpu.SemaphoreType.DMA((voxels // KB + chunks * 2 + 2 + subsets,)),
            pltpu.SemaphoreType.DMA((copies,)),
            pltpu.SemaphoreType.DMA((copies,)),
        ],
        compiler_params=pltpu.CompilerParams(
            collective_id=0, has_side_effects=True, vmem_limit_bytes=56 * 2**20),
        name="sart",
    )(order, offsets.reshape(subsets), volume, measured, weights)
    return place(order, upd, mis)


def place_kernel(order_ref, upd_hbm, mis_hbm, out_upd, out_mis, sem):
    band = mis_hbm.shape[3]
    rows = upd_hbm.shape[0] // 4
    copies = []
    for i in range(4):
        at = pl.ds(i * rows, rows)
        copies.append(pltpu.make_async_copy(upd_hbm.at[at, :], out_upd.at[at, :], sem.at[i]))
    for t in range(mis_hbm.shape[0]):
        view = order_ref[t]
        for hi in range(2):
            copies.append(pltpu.make_async_copy(
                mis_hbm.at[t, hi], out_mis.at[view, :, pl.ds(hi * band, band)], sem.at[4 + t * 2 + hi]))
    for cp in copies:
        cp.start()
    for cp in copies:
        cp.wait()


def place(order, upd, mis):
    subsets, _, slices, band = mis.shape
    any_spec = pl.BlockSpec(memory_space=pl.ANY)
    return pl.pallas_call(
        place_kernel,
        out_shape=(jax.ShapeDtypeStruct(upd.shape, upd.dtype),
                   jax.ShapeDtypeStruct((subsets, slices, 2 * band), mis.dtype)),
        in_specs=[pl.BlockSpec(memory_space=pltpu.SMEM), any_spec, any_spec],
        out_specs=(any_spec, any_spec),
        scratch_shapes=[pltpu.SemaphoreType.DMA((8,))],
        name="place",
    )(order, upd, mis)


def solution(mesh):
    placed = (
        P(None, "slab"),
        P("view", None, None),
        P("view", "slab", None),
        P("view", "slab"),
        P("view"),
    )
    return jax.shard_map(
        per_device,
        mesh=mesh,
        in_specs=placed,
        out_specs=(P(None, "slab"), P("view", None, None)),
        check_vma=False,
    )
```

```python
import jax
import jax.numpy as jnp
from jax import lax
from jax.experimental import pallas as pl
from jax.experimental.pallas import tpu as pltpu
from jax.sharding import PartitionSpec as P

RELAXATION = 0.9
MESH = pl.DeviceIdType.MESH
CHUNKS = 2
LANES = 128
KB = 1024
ORDER = (0, 1) + (0, 1, 0, 1, 0, 0, 1, 1, 0, 1, 0, 1, 0, 1, 0, 1, 0, 1) * 2


def kernel(chunks, order_ref, off_ref, vol_hbm, meas_hbm, w_hbm, upd_hbm, mis_hbm,
           wv, vol, meas, acc, bandb, x1, xo, fs, fr, gs, gr, cor, rsum, csum,
           bk, rc, ry0, rx0, ry1, rx1, obuf, mis, local_sem, send_sem, recv_sem):
    slices, voxels = vol.shape
    rows = slices // chunks
    band = wv.shape[2]
    subsets = 2
    half = voxels // 2 // LANES
    nb = band // LANES

    s = lax.axis_index("slab")
    v = lax.axis_index("view")
    core = lax.rem(v, 2)
    xh = lax.rem(v // 2, 2)
    y = v // 4
    xl = lax.rem(s, 2)
    z = s // 2

    def slab_dev(other):
        return {"slab": other, "view": v}

    def view_dev(other):
        return {"slab": s, "view": other}

    dev_core = view_dev(v + 1 - 2 * core)

    dev_x = view_dev(v + 2 - 4 * xh)

    def turned(dy):
        return lax.rem(y + dy, 4)

    def dev_y(dy):
        return view_dev(v + 4 * (turned(dy) - y))

    s_mate = s + 1 - 2 * xl
    dev_mate = slab_dev(s_mate)
    dev_z = [None] + [slab_dev(lax.rem(z + k, 4) * 2 + xl) for k in (1, 2, 3)]

    used = [0]
    pending = []

    def remote(src, dst, dev, arrives=None):
        at = used[0]
        used[0] += 1
        cp = pltpu.make_async_remote_copy(
            src_ref=src, dst_ref=dst, send_sem=send_sem.at[at], recv_sem=recv_sem.at[at],
            device_id=dev, device_id_type=MESH)
        cp.start()
        pending.append(cp)
        if arrives is None:
            return cp
        return pltpu.make_async_remote_copy(
            src_ref=src, dst_ref=arrives, send_sem=send_sem.at[at], recv_sem=recv_sem.at[at],
            device_id=dev, device_id_type=MESH)

    steps = voxels // KB
    def w_copy(i):
        at = pl.ds(i * KB, KB)
        return pltpu.make_async_copy(w_hbm.at[:, at, :], wv.at[:, at, :], local_sem.at[i])
    vol_copies = []
    for c in range(chunks):
        at = pl.ds(c * rows, rows)
        cp = pltpu.make_async_copy(vol_hbm.at[at, :], vol.at[at, :], local_sem.at[steps + c])
        cp.start()
        vol_copies.append(cp)
        if c == 0:
            for i in range(steps):
                w_copy(i).start()
    meas_copies = []
    for hi in range(2):
        col = pl.multiple_of(hi * band + s * LANES, LANES)
        cp = pltpu.make_async_copy(meas_hbm.at[:, :, pl.ds(col, LANES)], meas.at[hi],
                                   local_sem.at[steps + chunks + hi])
        cp.start()
        meas_copies.append(cp)

    barrier = pltpu.get_barrier_semaphore()
    for k in range(1, 8):
        pl.semaphore_signal(barrier, inc=1, device_id=slab_dev(lax.rem(s + k, 8)), device_id_type=MESH)
    pl.semaphore_signal(barrier, inc=1, device_id=dev_core, device_id_type=MESH)
    for dev in (dev_x, dev_y(1), dev_y(2), dev_y(3)):
        pl.semaphore_signal(barrier, inc=1, device_id=dev, device_id_type=MESH)

    column = lax.broadcasted_iota(jnp.int32, (8, LANES), 1) + s * LANES
    column = column.astype(jnp.float32)

    out_copies = []
    gathered = [[], []]

    def chain(c):
        at_rows = pl.ds(c * rows, rows)
        ext = 8 if c == 0 else 0
        m = rows + 2 * ext
        r = rows + ext
        rr = pl.ds(0, r)
        only = pl.ds(0, rows)
        for t in range(subsets):
            view_t = order_ref[t]
            off = off_ref[view_t]
            shift = jnp.where(off >= band, 0, off)
            if t == 0:
                vol_copies[c].wait()

            def forward(i, carry):
                at = pl.ds(pl.multiple_of(i * KB, KB), KB)
                if t == 0:
                    xk = vol[at_rows, at]
                else:
                    xk = jnp.concatenate(
                        [x1[c, i * (KB // LANES) + j] for j in range(KB // LANES)], axis=1)
                xk = xk.astype(jnp.bfloat16)
                if ext:
                    xk = jnp.concatenate([xk, jnp.ones((2 * ext, KB), jnp.bfloat16)], axis=0)
                if t == 0 and c == 0:
                    w_copy(i).wait()
                    wk = jnp.where(view_t == 0, wv[0, at, :], wv[1, at, :])
                else:
                    wk = wv[view_t, at, :]
                acc[c, pl.ds(0, m), :] += jnp.dot(xk, wk, preferred_element_type=jnp.float32)
                return carry

            acc[c, pl.ds(0, m), :] = jnp.zeros((m, band), jnp.float32)
            if t == 0:
                lax.fori_loop(0, steps, forward, 0)
            else:

                def joined(i, carry):
                    return forward(lax.rem(core + i // 2, 2) * 2 + lax.rem(1 + i, 2), carry)

                lax.fori_loop(0, 1, joined, 0)
                pass_on_rest()
                lax.fori_loop(1, 2, joined, 0)
                yield
                core_in[0].wait_recv()
                core_in[1].wait_recv()
                lax.fori_loop(2, 3, joined, 0)
                core_in[2].wait_recv()
                lax.fori_loop(3, 4, joined, 0)
            if t == 0 and c == 0:
                pl.semaphore_wait(barrier, 12)
            folded = pltpu.roll(acc[c, rr, :], shift, 1)
            if ext:
                tail = folded[rows:, :]
                kind = lax.broadcasted_iota(jnp.int32, tail.shape, 0)
                tail = jnp.where(kind < 4, tail, off.astype(jnp.float32))
            for b in range(nb):
                fs[t, c, b, only, :] = folded[:rows, b * LANES:(b + 1) * LANES]
                if ext:
                    fs[t, c, b, pl.ds(rows, ext), :] = tail[:, b * LANES:(b + 1) * LANES]
            arrivals = []
            for k in range(1, 8):
                peer = lax.rem(s + k, 8)
                arrivals.append(remote(fs.at[t, c, peer, rr], fr.at[t, c, k, rr], slab_dev(peer)))
            yield
            fr[t, c, 0, rr, :] = fs[t, c, s, rr, :]
            for cp in arrivals:
                cp.wait_recv()
            if t == 0 and c == 0:
                for cp in meas_copies:
                    cp.wait()
            low = jnp.zeros((rows, LANES), jnp.float32)
            high = jnp.zeros((rows, LANES), jnp.float32)
            masks = []
            for k in range(8):
                offs = fr[t, 0, k, pl.ds(rows + 4, 1), :]
                masks.append(column[0:1, :] >= offs)
            if ext:
                rlow = jnp.zeros((1, LANES), jnp.float32)
                rhigh = jnp.zeros((1, LANES), jnp.float32)
                for k in range(8):
                    part = fr[t, c, k, pl.ds(rows, 1), :]
                    rlow += jnp.where(masks[k], part, 0.0)
                    rhigh += jnp.where(masks[k], 0.0, part)
                rsum[t, 0] = jnp.broadcast_to(jnp.maximum(rlow, 1.0), (8, LANES))
                rsum[t, 1] = jnp.broadcast_to(jnp.maximum(rhigh, 1.0), (8, LANES))
            for k in range(8):
                part = fr[t, c, k, only, :]
                low += jnp.where(masks[k], part, 0.0)
                high += jnp.where(masks[k], 0.0, part)
            seen_low = meas[0, view_t, at_rows, :].astype(jnp.float32)
            seen_high = meas[1, view_t, at_rows, :].astype(jnp.float32)
            low = (seen_low - low) / rsum[t, 0, pl.ds(0, 1), :]
            high = (seen_high - high) / rsum[t, 1, pl.ds(0, 1), :]
            cor[t, 0, at_rows, :] = low
            cor[t, 1, at_rows, :] = high
            arrivals = []
            for k in range(8):
                piece = jnp.where(masks[k], low, high)
                if k == 0:
                    gr[t, c, s] = piece
                else:
                    gs[t, c, k] = piece
                    arrivals.append(remote(
                        gs.at[t, c, k], gr.at[t, c, s], slab_dev(lax.rem(s + 8 - k, 8)),
                        gr.at[t, c, lax.rem(s + k, 8)]))
            yield
            for cp in arrivals:
                cp.wait_recv()
            if c == chunks - 1:
                def cols(slab):
                    at = pl.ds(pl.multiple_of(slab * LANES, LANES), LANES)
                    return mis.at[t, :, :, at]
                at = pl.ds(pl.multiple_of(s * LANES, LANES), LANES)
                for hi in range(2):
                    mis[t, hi, :, at] = cor[t, hi]
                mate_in = remote(cor.at[t], cols(s), dev_mate, cols(s_mate))
                for k in (1, 2, 3):
                    far = lax.rem(z + 4 - k, 4) * 2 + xl
                    gathered[t].append((remote(cor.at[t], cols(s), dev_z[k], cols(far))))
            g = jnp.concatenate([gr[t, c, b] for b in range(nb)], axis=1)
            g = pltpu.roll(g, jnp.where(shift == 0, 0, band - shift), 1).astype(jnp.bfloat16)
            bandb[c, only, :] = g
            if ext:
                bandb[c, pl.ds(rows, 2 * ext), :] = jnp.ones((2 * ext, band), jnp.bfloat16)

            def backward(base):
                def step(n, carry):
                    vb = base + n * (KB // LANES)
                    wk = wv[view_t, pl.ds(pl.multiple_of(vb * LANES, LANES), KB), :]
                    res = lax.dot_general(bandb[c, pl.ds(0, m), :], wk, (((1,), (1,)), ((), ())),
                                          preferred_element_type=jnp.float32)
                    for j in range(KB // LANES):
                        bk[t, c, vb + j, rr, :] = res[:r, j * LANES:(j + 1) * LANES]
                    return carry
                lax.fori_loop(0, half * LANES // KB, step, 0)

            theirs = (1 - core) * half
            mine = core * half
            backward(theirs)
            core_in = remote(bk.at[t, c, pl.ds(theirs, half), rr], rc.at[t, c, :, rr], dev_core)
            yield
            backward(mine)
            yield
            if c == chunks - 1:
                mate_in.wait_recv()
                for k in (1, 2, 3):
                    far = lax.rem(z + 4 - k, 4) * 2 + 1 - xl
                    gathered[t].append((remote(cols(s_mate), cols(s_mate), dev_z[k], cols(far))))
            core_in.wait_recv()

            def add(block, *others):
                total = bk[t, c, mine + block, rr, :]
                for other in others:
                    total += other[...]
                bk[t, c, mine + block, rr, :] = total

            def theirs_of(block):
                return rc.at[t, c, block, rr]

            other_x = 8 + (1 - xh) * 4
            own_x = 8 + xh * 4
            ins_y, ins_x = [], []
            for j in range(4):
                add(other_x + j, theirs_of(other_x + j))
            ins_x.append(remote(bk.at[t, c, pl.ds(mine + other_x, 4), rr], rx1.at[t, c, :, rr], dev_x))
            for k in (2, 1, 3):
                block = turned(k) * 2
                for j in range(2):
                    add(block + j, theirs_of(block + j))
                ins_y.append(remote(bk.at[t, c, pl.ds(mine + block, 2), rr],
                                    ry0.at[t, c, k - 1, :, rr], dev_y(k)))
            yield
            for cp in ins_x:
                cp.wait_recv()
            last_x, last_y = [], []
            for k in (2, 1, 3, 0):
                block = own_x + turned(k)
                add(block, theirs_of(block), rx1.at[t, c, turned(k), rr])
                if k:
                    last_y.append(remote(bk.at[t, c, mine + block, rr], ry1.at[t, c, k - 1, rr], dev_y(k)))
            for cp in ins_y:
                cp.wait_recv()
            for far in (1, 0):
                at = 1 - xh if far else xh
                block = y * 2 + at
                add(block, theirs_of(block), *[ry0.at[t, c, k, at, rr] for k in range(3)])
                if far:
                    last_x.append(remote(bk.at[t, c, mine + block, rr], rx0.at[t, c, rr], dev_x))
            yield
            x_new = x1 if t == 0 else xo

            def renew(block, j, *others):
                vb = mine + block
                total = bk[t, c, vb, rr, :]
                for other in others:
                    total += other[...]
                if ext:
                    csum[t, j] = total[rows:, :]
                if t == 0:
                    old = vol[at_rows, pl.ds(pl.multiple_of(vb * LANES, LANES), LANES)]
                else:
                    old = x1[c, vb]
                x_new[c, vb] = old + RELAXATION * total[:rows, :] / csum[t, j, pl.ds(0, 1), :]

            def send(at, dev, arrives):
                return remote(at, at, dev, arrives)

            def span(block, count, x_new=x_new):
                return x_new.at[c, pl.ds(mine + block, count)]

            for cp in last_y:
                cp.wait_recv()
            renew(own_x + y, 1, *[ry1.at[t, c, k, rr] for k in range(3)])
            ins_y = [send(span(own_x + y, 1), dev_y(k), span(own_x + turned(4 - k), 1)) for k in (2, 1, 3)]
            for cp in last_x:
                cp.wait_recv()
            renew(y * 2 + xh, 0, rx0.at[t, c, rr])
            ins_x = [send(span(y * 2 + xh, 1), dev_x, span(y * 2 + 1 - xh, 1))]
            yield
            for cp in ins_y:
                cp.wait_recv()
            last_x = [send(span(own_x, 4), dev_x, span(other_x, 4))]
            for cp in ins_x:
                cp.wait_recv()
            last_y = [send(span(y * 2, 2), dev_y(k), span(turned(4 - k) * 2, 2)) for k in (2, 1, 3)]

            def pass_on(block, count, x_new=x_new):
                return send(x_new.at[c, pl.ds(mine + block, count)], dev_core,
                            x_new.at[c, pl.ds(theirs + block, count)])

            core_in = [pass_on(own_x, 4)]
            yield
            for cp in last_x:
                cp.wait_recv()
            core_in.append(pass_on(other_x, 4))

            def pass_on_rest(last_y=last_y, core_in=core_in, pass_on=pass_on):
                for cp in last_y:
                    cp.wait_recv()
                core_in.append(pass_on(0, 8))

        def lay_out(base):
            for j in range(half // 2):
                at = pl.ds(pl.multiple_of((base + j) * LANES, LANES), LANES)
                obuf[at_rows, at] = xo[c, base + j]

        lay_out(mine + 8)
        pass_on_rest()
        lay_out(mine)
        yield
        core_in[0].wait_recv()
        core_in[1].wait_recv()
        lay_out(theirs + 8)
        core_in[2].wait_recv()
        lay_out(theirs)
        done = pltpu.make_async_copy(obuf.at[at_rows, :], upd_hbm.at[at_rows, :],
                                     local_sem.at[steps + chunks + 2 + subsets + c])
        done.start()
        out_copies.append(done)

    live = [chain(c) for c in range(chunks)]
    for c in ORDER:
        next(live[c], None)
    for t in range(subsets):
        for cp in gathered[t]:
            cp.wait_recv()
        cp = pltpu.make_async_copy(mis.at[t], mis_hbm.at[t], local_sem.at[steps + chunks + 2 + t])
        cp.start()
        out_copies.append(cp)
    for cp in out_copies:
        cp.wait()
    for cp in pending:
        cp.wait_send()


def per_device(volume, measured, weights, offsets, order):
    subsets, voxels, band = weights.shape
    slices = volume.shape[0]
    cols = measured.shape[2]
    chunks = CHUNKS
    rows = slices // chunks
    r = rows + 8
    nb = band // LANES
    vb = voxels // LANES
    f32 = jnp.float32
    copies = 34 * subsets * chunks + 7 * subsets
    any_spec = pl.BlockSpec(memory_space=pl.ANY)
    smem = pl.BlockSpec(memory_space=pltpu.SMEM)
    upd, mis = pl.pallas_call(
        lambda *refs: kernel(chunks, *refs),
        out_shape=(jax.ShapeDtypeStruct((slices, voxels), f32),
                   jax.ShapeDtypeStruct((subsets, 2, slices, band), f32)),
        in_specs=[smem, smem, any_spec, any_spec, any_spec],
        out_specs=(any_spec, any_spec),
        scratch_shapes=[
            pltpu.VMEM((subsets, voxels, band), jnp.bfloat16),
            pltpu.VMEM((slices, voxels), f32),
            pltpu.VMEM((2, subsets, slices, LANES), jnp.bfloat16),
            pltpu.VMEM((chunks, rows + 16, band), f32),
            pltpu.VMEM((chunks, rows + 16, band), jnp.bfloat16),
            pltpu.VMEM((chunks, vb, rows, LANES), f32),
            pltpu.VMEM((chunks, vb, rows, LANES), f32),
            pltpu.VMEM((subsets, chunks, nb, r, LANES), f32),
            pltpu.VMEM((subsets, chunks, nb, r, LANES), f32),
            pltpu.VMEM((subsets, chunks, nb, rows, LANES), f32),
            pltpu.VMEM((subsets, chunks, nb, rows, LANES), f32),
            pltpu.VMEM((subsets, 2, slices, LANES), f32),
            pltpu.VMEM((subsets, 2, 8, LANES), f32),
            pltpu.VMEM((subsets, 2, 8, LANES), f32),
            pltpu.VMEM((subsets, chunks, vb, r, LANES), f32),
            pltpu.VMEM((subsets, chunks, vb // 2, r, LANES), f32),
            pltpu.VMEM((subsets, chunks, 3, 2, r, LANES), f32),
            pltpu.VMEM((subsets, chunks, r, LANES), f32),
            pltpu.VMEM((subsets, chunks, 3, r, LANES), f32),
            pltpu.VMEM((subsets, chunks, 4, r, LANES), f32),
            pltpu.VMEM((slices, voxels), f32),
            pltpu.VMEM((subsets, 2, slices, band), f32),
            pltpu.SemaphoreType.DMA((voxels // KB + chunks * 2 + 2 + subsets,)),
            pltpu.SemaphoreType.DMA((copies,)),
            pltpu.SemaphoreType.DMA((copies,)),
        ],
        compiler_params=pltpu.CompilerParams(
            collective_id=0, has_side_effects=True, vmem_limit_bytes=56 * 2**20),
        name="sart",
    )(order, offsets.reshape(subsets), volume, measured, weights)
    return place(order, upd, mis)


def place_kernel(order_ref, upd_hbm, mis_hbm, out_upd, out_mis, upd, mis, sem):
    band = mis.shape[3]
    rows = upd.shape[0] // 4
    moves = []
    for t in range(mis.shape[0]):
        view = order_ref[t]
        for hi in range(2):
            moves.append((mis_hbm.at[t, hi], mis.at[t, hi], out_mis.at[view, :, pl.ds(hi * band, band)]))
    for i in range(4):
        at = pl.ds(i * rows, rows)
        moves.append((upd_hbm.at[at, :], upd.at[at, :], out_upd.at[at, :]))
    loads = [pltpu.make_async_copy(a, b, sem.at[0, i]) for i, (a, b, _) in enumerate(moves)]
    stores = [pltpu.make_async_copy(b, c, sem.at[1, i]) for i, (_, b, c) in enumerate(moves)]
    for cp in loads:
        cp.start()
    for load, store in zip(loads, stores):
        load.wait()
        store.start()
    for cp in stores:
        cp.wait()


def place(order, upd, mis):
    subsets, _, slices, band = mis.shape
    any_spec = pl.BlockSpec(memory_space=pl.ANY)
    return pl.pallas_call(
        place_kernel,
        out_shape=(jax.ShapeDtypeStruct(upd.shape, upd.dtype),
                   jax.ShapeDtypeStruct((subsets, slices, 2 * band), mis.dtype)),
        in_specs=[pl.BlockSpec(memory_space=pltpu.SMEM), any_spec, any_spec],
        out_specs=(any_spec, any_spec),
        scratch_shapes=[pltpu.VMEM(upd.shape, upd.dtype), pltpu.VMEM(mis.shape, mis.dtype),
                        pltpu.SemaphoreType.DMA((2, 8))],
        name="place",
    )(order, upd, mis)


def solution(mesh):
    placed = (
        P(None, "slab"),
        P("view", None, None),
        P("view", "slab", None),
        P("view", "slab"),
        P("view"),
    )
    return jax.shard_map(
        per_device,
        mesh=mesh,
        in_specs=placed,
        out_specs=(P(None, "slab"), P("view", None, None)),
        check_vma=False,
    )
```

```python
import jax
import jax.numpy as jnp
from jax import lax
from jax.experimental import pallas as pl
from jax.experimental.pallas import tpu as pltpu
from jax.sharding import PartitionSpec as P

RELAXATION = 0.9
MESH = pl.DeviceIdType.MESH
CHUNKS = 2
LANES = 128
KB = 1024
SLAB_PEERS = ((2, 1), (1, 1), (3, 1), (2, 0), (1, 0), (3, 0), (0, 1))
ORDER = (0, 1) + (0, 1, 0, 1, 0, 0, 1, 1, 0, 1, 0, 1, 0, 1, 0, 0, 1, 1) * 2


def kernel(chunks, order_ref, off_ref, vol_hbm, meas_hbm, w_hbm, obuf, mis,
           wv, vol, meas, acc, bandb, x1, xo, fs, fr, gs, gr, cor, rsum, csum,
           bk, rc, ry0, rx0, ry1, rx1, local_sem, send_sem, recv_sem):
    slices, voxels = vol.shape
    rows = slices // chunks
    band = wv.shape[2]
    subsets = 2
    half = voxels // 2 // LANES
    nb = band // LANES

    s = lax.axis_index("slab")
    v = lax.axis_index("view")
    core = lax.rem(v, 2)
    xh = lax.rem(v // 2, 2)
    y = v // 4
    xl = lax.rem(s, 2)
    z = s // 2

    def slab_dev(other):
        return {"slab": other, "view": v}

    def view_dev(other):
        return {"slab": s, "view": other}

    dev_core = view_dev(v + 1 - 2 * core)

    dev_x = view_dev(v + 2 - 4 * xh)

    def turned(dy):
        return lax.rem(y + dy, 4)

    def dev_y(dy):
        return view_dev(v + 4 * (turned(dy) - y))

    s_mate = s + 1 - 2 * xl
    dev_mate = slab_dev(s_mate)

    def across(dz, dx):
        return lax.rem(z + dz, 4) * 2 + (1 - xl if dx else xl)

    dev_z = [None] + [slab_dev(lax.rem(z + k, 4) * 2 + xl) for k in (1, 2, 3)]

    used = [0]
    pending = []

    def remote(src, dst, dev, arrives=None):
        at = used[0]
        used[0] += 1
        cp = pltpu.make_async_remote_copy(
            src_ref=src, dst_ref=dst, send_sem=send_sem.at[at], recv_sem=recv_sem.at[at],
            device_id=dev, device_id_type=MESH)
        cp.start()
        pending.append(cp)
        if arrives is None:
            return cp
        return pltpu.make_async_remote_copy(
            src_ref=src, dst_ref=arrives, send_sem=send_sem.at[at], recv_sem=recv_sem.at[at],
            device_id=dev, device_id_type=MESH)

    steps = voxels // KB
    def w_copy(i):
        at = pl.ds(i * KB, KB)
        return pltpu.make_async_copy(w_hbm.at[:, at, :], wv.at[:, at, :], local_sem.at[i])
    vol_copies = []
    for c in range(chunks):
        at = pl.ds(c * rows, rows)
        cp = pltpu.make_async_copy(vol_hbm.at[at, :], vol.at[at, :], local_sem.at[steps + c])
        cp.start()
        vol_copies.append(cp)
        if c == 0:
            for i in range(steps):
                w_copy(i).start()
    meas_copies = []
    for hi in range(2):
        col = pl.multiple_of(hi * band + s * LANES, LANES)
        cp = pltpu.make_async_copy(meas_hbm.at[:, :, pl.ds(col, LANES)], meas.at[hi],
                                   local_sem.at[steps + chunks + hi])
        cp.start()
        meas_copies.append(cp)

    barrier = pltpu.get_barrier_semaphore()
    for k in range(1, 8):
        pl.semaphore_signal(barrier, inc=1, device_id=slab_dev(lax.rem(s + k, 8)), device_id_type=MESH)
    pl.semaphore_signal(barrier, inc=1, device_id=dev_core, device_id_type=MESH)
    for dev in (dev_x, dev_y(1), dev_y(2), dev_y(3)):
        pl.semaphore_signal(barrier, inc=1, device_id=dev, device_id_type=MESH)

    column = lax.broadcasted_iota(jnp.int32, (8, LANES), 1) + s * LANES
    column = column.astype(jnp.float32)

    out_copies = []
    gathered = [[], []]

    def chain(c):
        at_rows = pl.ds(c * rows, rows)
        ext = 8 if c == 0 else 0
        m = rows + 2 * ext
        r = rows + ext
        rr = pl.ds(0, r)
        only = pl.ds(0, rows)
        for t in range(subsets):
            view_t = order_ref[t]
            off = off_ref[view_t]
            shift = jnp.where(off >= band, 0, off)
            if t == 0:
                vol_copies[c].wait()

            def forward(i, carry):
                at = pl.ds(pl.multiple_of(i * KB, KB), KB)
                if t == 0:
                    xk = vol[at_rows, at]
                else:
                    xk = jnp.concatenate(
                        [x1[c, i * (KB // LANES) + j] for j in range(KB // LANES)], axis=1)
                xk = xk.astype(jnp.bfloat16)
                if ext:
                    xk = jnp.concatenate([xk, jnp.ones((2 * ext, KB), jnp.bfloat16)], axis=0)
                if t == 0 and c == 0:
                    w_copy(i).wait()
                    wk = jnp.where(view_t == 0, wv[0, at, :], wv[1, at, :])
                else:
                    wk = wv[view_t, at, :]
                acc[c, pl.ds(0, m), :] += jnp.dot(xk, wk, preferred_element_type=jnp.float32)
                return carry

            acc[c, pl.ds(0, m), :] = jnp.zeros((m, band), jnp.float32)
            if t == 0:
                lax.fori_loop(0, steps, forward, 0)
            else:

                def joined(i, carry):
                    return forward(lax.rem(core + i // 2, 2) * 2 + lax.rem(1 + i, 2), carry)

                lax.fori_loop(0, 1, joined, 0)
                pass_on_rest()
                lax.fori_loop(1, 2, joined, 0)
                yield
                core_in[0].wait_recv()
                core_in[1].wait_recv()
                lax.fori_loop(2, 3, joined, 0)
                core_in[2].wait_recv()
                lax.fori_loop(3, 4, joined, 0)
            if t == 0 and c == 0:
                pl.semaphore_wait(barrier, 12)
            folded = pltpu.roll(acc[c, rr, :], shift, 1)
            if ext:
                tail = folded[rows:, :]
                kind = lax.broadcasted_iota(jnp.int32, tail.shape, 0)
                tail = jnp.where(kind < 4, tail, off.astype(jnp.float32))
            for b in range(nb):
                fs[t, c, b, only, :] = folded[:rows, b * LANES:(b + 1) * LANES]
                if ext:
                    fs[t, c, b, pl.ds(rows, ext), :] = tail[:, b * LANES:(b + 1) * LANES]
            arrivals = []
            for k, (dz, dx) in enumerate(SLAB_PEERS, 1):
                peer = across(dz, dx)
                arrivals.append(remote(fs.at[t, c, peer, rr], fr.at[t, c, k, rr], slab_dev(peer)))
            yield
            fr[t, c, 0, rr, :] = fs[t, c, s, rr, :]
            for cp in arrivals:
                cp.wait_recv()
            if t == 0 and c == 0:
                for cp in meas_copies:
                    cp.wait()
            low = jnp.zeros((rows, LANES), jnp.float32)
            high = jnp.zeros((rows, LANES), jnp.float32)
            masks = []
            for k in range(8):
                offs = fr[t, 0, k, pl.ds(rows + 4, 1), :]
                masks.append(column[0:1, :] >= offs)
            if ext:
                rlow = jnp.zeros((1, LANES), jnp.float32)
                rhigh = jnp.zeros((1, LANES), jnp.float32)
                for k in range(8):
                    part = fr[t, c, k, pl.ds(rows, 1), :]
                    rlow += jnp.where(masks[k], part, 0.0)
                    rhigh += jnp.where(masks[k], 0.0, part)
                rsum[t, 0] = jnp.broadcast_to(jnp.maximum(rlow, 1.0), (8, LANES))
                rsum[t, 1] = jnp.broadcast_to(jnp.maximum(rhigh, 1.0), (8, LANES))
            for k in range(8):
                part = fr[t, c, k, only, :]
                low += jnp.where(masks[k], part, 0.0)
                high += jnp.where(masks[k], 0.0, part)
            seen_low = meas[0, view_t, at_rows, :].astype(jnp.float32)
            seen_high = meas[1, view_t, at_rows, :].astype(jnp.float32)
            low = (seen_low - low) / rsum[t, 0, pl.ds(0, 1), :]
            high = (seen_high - high) / rsum[t, 1, pl.ds(0, 1), :]
            cor[t, 0, at_rows, :] = low
            cor[t, 1, at_rows, :] = high
            arrivals = []
            for k, (dz, dx) in enumerate(SLAB_PEERS, 1):
                gs[t, c, k] = jnp.where(masks[k], low, high)
                arrivals.append(remote(
                    gs.at[t, c, k], gr.at[t, c, s], slab_dev(across(4 - dz, dx)),
                    gr.at[t, c, across(dz, dx)]))
            gr[t, c, s] = jnp.where(masks[0], low, high)
            yield
            for cp in arrivals:
                cp.wait_recv()
            if c == chunks - 1:
                def cols(slab):
                    at = pl.ds(pl.multiple_of(slab * LANES, LANES), LANES)
                    return mis.at[t, :, :, at]
                at = pl.ds(pl.multiple_of(s * LANES, LANES), LANES)
                for hi in range(2):
                    mis[t, hi, :, at] = cor[t, hi]
                for k in (1, 2, 3):
                    far = lax.rem(z + 4 - k, 4) * 2 + xl
                    gathered[t].append((remote(cor.at[t], cols(s), dev_z[k], cols(far))))
            g = jnp.concatenate([gr[t, c, b] for b in range(nb)], axis=1)
            g = pltpu.roll(g, jnp.where(shift == 0, 0, band - shift), 1).astype(jnp.bfloat16)
            bandb[c, only, :] = g
            if ext:
                bandb[c, pl.ds(rows, 2 * ext), :] = jnp.ones((2 * ext, band), jnp.bfloat16)

            def backward(base):
                def step(n, carry):
                    vb = base + n * (KB // LANES)
                    wk = wv[view_t, pl.ds(pl.multiple_of(vb * LANES, LANES), KB), :]
                    res = lax.dot_general(bandb[c, pl.ds(0, m), :], wk, (((1,), (1,)), ((), ())),
                                          preferred_element_type=jnp.float32)
                    for j in range(KB // LANES):
                        bk[t, c, vb + j, rr, :] = res[:r, j * LANES:(j + 1) * LANES]
                    return carry
                lax.fori_loop(0, half * LANES // KB, step, 0)

            theirs = (1 - core) * half
            mine = core * half
            backward(theirs)
            core_in = remote(bk.at[t, c, pl.ds(theirs, half), rr], rc.at[t, c, :, rr], dev_core)
            yield
            backward(mine)
            yield
            core_in.wait_recv()

            def add(block, *others):
                total = bk[t, c, mine + block, rr, :]
                for other in others:
                    total += other[...]
                bk[t, c, mine + block, rr, :] = total

            def theirs_of(block):
                return rc.at[t, c, block, rr]

            other_x = 8 + (1 - xh) * 4
            own_x = 8 + xh * 4
            ins_y, ins_x = [], []
            for j in range(4):
                add(other_x + j, theirs_of(other_x + j))
            ins_x.append(remote(bk.at[t, c, pl.ds(mine + other_x, 4), rr], rx1.at[t, c, :, rr], dev_x))
            for k in (2, 1, 3):
                block = turned(k) * 2
                for j in range(2):
                    add(block + j, theirs_of(block + j))
                ins_y.append(remote(bk.at[t, c, pl.ds(mine + block, 2), rr],
                                    ry0.at[t, c, k - 1, :, rr], dev_y(k)))
            yield
            for cp in ins_x:
                cp.wait_recv()
            last_x, last_y = [], []
            for k in (2, 1, 3, 0):
                block = own_x + turned(k)
                add(block, theirs_of(block), rx1.at[t, c, turned(k), rr])
                if k:
                    last_y.append(remote(bk.at[t, c, mine + block, rr], ry1.at[t, c, k - 1, rr], dev_y(k)))
            for cp in ins_y:
                cp.wait_recv()
            for far in (1, 0):
                at = 1 - xh if far else xh
                block = y * 2 + at
                add(block, theirs_of(block), *[ry0.at[t, c, k, at, rr] for k in range(3)])
                if far:
                    last_x.append(remote(bk.at[t, c, mine + block, rr], rx0.at[t, c, rr], dev_x))
            if c == chunks - 1:
                mate_in = remote(cor.at[t], cols(s), dev_mate, cols(s_mate))
            yield
            x_new = x1 if t == 0 else xo

            def renew(block, j, *others):
                vb = mine + block
                total = bk[t, c, vb, rr, :]
                for other in others:
                    total += other[...]
                if ext:
                    csum[t, j] = total[rows:, :]
                if t == 0:
                    old = vol[at_rows, pl.ds(pl.multiple_of(vb * LANES, LANES), LANES)]
                else:
                    old = x1[c, vb]
                x_new[c, vb] = old + RELAXATION * total[:rows, :] / csum[t, j, pl.ds(0, 1), :]

            def send(at, dev, arrives):
                return remote(at, at, dev, arrives)

            def span(block, count, x_new=x_new):
                return x_new.at[c, pl.ds(mine + block, count)]

            for cp in last_y:
                cp.wait_recv()
            renew(own_x + y, 1, *[ry1.at[t, c, k, rr] for k in range(3)])
            ins_y = [send(span(own_x + y, 1), dev_y(k), span(own_x + turned(4 - k), 1)) for k in (2, 1, 3)]
            for cp in last_x:
                cp.wait_recv()
            renew(y * 2 + xh, 0, rx0.at[t, c, rr])
            ins_x = [send(span(y * 2 + xh, 1), dev_x, span(y * 2 + 1 - xh, 1))]
            if c == chunks - 1:
                mate_in.wait_recv()
                for k in (1, 2, 3):
                    far = lax.rem(z + 4 - k, 4) * 2 + 1 - xl
                    gathered[t].append((remote(cols(s_mate), cols(s_mate), dev_z[k], cols(far))))
            yield
            for cp in ins_y:
                cp.wait_recv()
            last_x = [send(span(own_x, 4), dev_x, span(other_x, 4))]
            for cp in ins_x:
                cp.wait_recv()
            last_y = [send(span(y * 2, 2), dev_y(k), span(turned(4 - k) * 2, 2)) for k in (2, 1, 3)]

            def pass_on(block, count, x_new=x_new):
                return send(x_new.at[c, pl.ds(mine + block, count)], dev_core,
                            x_new.at[c, pl.ds(theirs + block, count)])

            core_in = [pass_on(own_x, 4)]
            yield
            for cp in last_x:
                cp.wait_recv()
            core_in.append(pass_on(other_x, 4))

            def pass_on_rest(last_y=last_y, core_in=core_in, pass_on=pass_on):
                for cp in last_y:
                    cp.wait_recv()
                core_in.append(pass_on(0, 8))

        def lay_out(base):
            for j in range(half // 2):
                at = pl.ds(pl.multiple_of((base + j) * LANES, LANES), LANES)
                obuf[at_rows, at] = xo[c, base + j]

        lay_out(mine + 8)
        pass_on_rest()
        lay_out(mine)
        yield
        core_in[0].wait_recv()
        core_in[1].wait_recv()
        lay_out(theirs + 8)
        core_in[2].wait_recv()
        lay_out(theirs)

    live = [chain(c) for c in range(chunks)]
    for c in ORDER:
        next(live[c], None)
    for t in range(subsets):
        for cp in gathered[t]:
            cp.wait_recv()
    for cp in out_copies:
        cp.wait()
    for cp in pending:
        cp.wait_send()


def per_device(volume, measured, weights, offsets, order):
    subsets, voxels, band = weights.shape
    slices = volume.shape[0]
    cols = measured.shape[2]
    chunks = CHUNKS
    rows = slices // chunks
    r = rows + 8
    nb = band // LANES
    vb = voxels // LANES
    f32 = jnp.float32
    copies = 34 * subsets * chunks + 7 * subsets
    hbm = pl.BlockSpec(memory_space=pltpu.HBM)
    smem = pl.BlockSpec(memory_space=pltpu.SMEM)
    upd, mis = pl.pallas_call(
        lambda *refs: kernel(chunks, *refs),
        out_shape=(pltpu.VMEM((slices, voxels), f32),
                   pltpu.VMEM((subsets, 2, slices, band), f32)),
        in_specs=[smem, smem, hbm, hbm, hbm],
        out_specs=(pl.BlockSpec(memory_space=pltpu.VMEM), pl.BlockSpec(memory_space=pltpu.VMEM)),
        scratch_shapes=[
            pltpu.VMEM((subsets, voxels, band), jnp.bfloat16),
            pltpu.VMEM((slices, voxels), f32),
            pltpu.VMEM((2, subsets, slices, LANES), jnp.bfloat16),
            pltpu.VMEM((chunks, rows + 16, band), f32),
            pltpu.VMEM((chunks, rows + 16, band), jnp.bfloat16),
            pltpu.VMEM((chunks, vb, rows, LANES), f32),
            pltpu.VMEM((chunks, vb, rows, LANES), f32),
            pltpu.VMEM((subsets, chunks, nb, r, LANES), f32),
            pltpu.VMEM((subsets, chunks, nb, r, LANES), f32),
            pltpu.VMEM((subsets, chunks, nb, rows, LANES), f32),
            pltpu.VMEM((subsets, chunks, nb, rows, LANES), f32),
            pltpu.VMEM((subsets, 2, slices, LANES), f32),
            pltpu.VMEM((subsets, 2, 8, LANES), f32),
            pltpu.VMEM((subsets, 2, 8, LANES), f32),
            pltpu.VMEM((subsets, chunks, vb, r, LANES), f32),
            pltpu.VMEM((subsets, chunks, vb // 2, r, LANES), f32),
            pltpu.VMEM((subsets, chunks, 3, 2, r, LANES), f32),
            pltpu.VMEM((subsets, chunks, r, LANES), f32),
            pltpu.VMEM((subsets, chunks, 3, r, LANES), f32),
            pltpu.VMEM((subsets, chunks, 4, r, LANES), f32),
            pltpu.SemaphoreType.DMA((voxels // KB + chunks * 2 + 2 + subsets,)),
            pltpu.SemaphoreType.DMA((copies,)),
            pltpu.SemaphoreType.DMA((copies,)),
        ],
        compiler_params=pltpu.CompilerParams(
            collective_id=0, has_side_effects=True, vmem_limit_bytes=56 * 2**20),
        name="sart",
    )(order, offsets.reshape(subsets), volume, measured, weights)
    return place(order, upd, mis)


def place_kernel(order_ref, upd, mis, out_upd, out_mis, sem):
    band = mis.shape[3]
    rows = upd.shape[0] // 4
    stores = []
    for t in range(mis.shape[0]):
        view = order_ref[t]
        for hi in range(2):
            stores.append(pltpu.make_async_copy(
                mis.at[t, hi], out_mis.at[view, :, pl.ds(hi * band, band)], sem.at[len(stores)]))
    for i in range(4):
        at = pl.ds(i * rows, rows)
        stores.append(pltpu.make_async_copy(upd.at[at, :], out_upd.at[at, :], sem.at[len(stores)]))
    for cp in stores:
        cp.start()
    for cp in stores:
        cp.wait()


def place(order, upd, mis):
    subsets, _, slices, band = mis.shape
    any_spec = pl.BlockSpec(memory_space=pl.ANY)
    return pl.pallas_call(
        place_kernel,
        out_shape=(jax.ShapeDtypeStruct(upd.shape, upd.dtype),
                   jax.ShapeDtypeStruct((subsets, slices, 2 * band), mis.dtype)),
        in_specs=[pl.BlockSpec(memory_space=pltpu.SMEM), pl.BlockSpec(memory_space=pltpu.VMEM), pl.BlockSpec(memory_space=pltpu.VMEM)],
        out_specs=(any_spec, any_spec),
        scratch_shapes=[pltpu.SemaphoreType.DMA((8,))],
        compiler_params=pltpu.CompilerParams(vmem_limit_bytes=2**20),
        name="place",
    )(order, pltpu.with_memory_space_constraint(upd, pltpu.VMEM),
      pltpu.with_memory_space_constraint(mis, pltpu.VMEM))


def solution(mesh):
    placed = (
        P(None, "slab"),
        P("view", None, None),
        P("view", "slab", None),
        P("view", "slab"),
        P("view"),
    )
    return jax.shard_map(
        per_device,
        mesh=mesh,
        in_specs=placed,
        out_specs=(P(None, "slab"), P("view", None, None)),
        check_vma=False,
    )
```

```python
import jax
import jax.numpy as jnp
from jax import lax
from jax.experimental import pallas as pl
from jax.experimental.pallas import tpu as pltpu
from jax.sharding import PartitionSpec as P

RELAXATION = 0.9
MESH = pl.DeviceIdType.MESH
CHUNKS = 2
LANES = 128
KB = 1024
SLAB_PEERS = ((2, 1), (1, 1), (3, 1), (2, 0), (1, 0), (3, 0), (0, 1))
ORDER = (0, 1) + (0, 1, 0, 1, 0, 0, 1, 1, 0, 1, 0, 1, 0, 1, 0, 0, 1, 1) * 2


def kernel(chunks, order_ref, off_ref, vol_hbm, meas_hbm, w_hbm, obuf, mis,
           wv, vol, meas, acc, bandb, x1, xo, fs, fr, gs, gr, cor, rsum, csum,
           bk, rc, ry0, rx0, ry1, rx1, local_sem, send_sem, recv_sem):
    slices, voxels = vol.shape
    rows = slices // chunks
    band = wv.shape[2]
    subsets = 2
    half = voxels // 2 // LANES
    nb = band // LANES

    s = lax.axis_index("slab")
    v = lax.axis_index("view")
    core = lax.rem(v, 2)
    xh = lax.rem(v // 2, 2)
    y = v // 4
    xl = lax.rem(s, 2)
    z = s // 2

    def slab_dev(other):
        return {"slab": other, "view": v}

    def view_dev(other):
        return {"slab": s, "view": other}

    dev_core = view_dev(v + 1 - 2 * core)

    dev_x = view_dev(v + 2 - 4 * xh)

    def turned(dy):
        return lax.rem(y + dy, 4)

    def dev_y(dy):
        return view_dev(v + 4 * (turned(dy) - y))

    s_mate = s + 1 - 2 * xl
    dev_mate = slab_dev(s_mate)

    def across(dz, dx):
        return lax.rem(z + dz, 4) * 2 + (1 - xl if dx else xl)

    dev_z = [None] + [slab_dev(lax.rem(z + k, 4) * 2 + xl) for k in (1, 2, 3)]

    used = [0]
    pending = []

    def remote(src, dst, dev, arrives=None):
        at = used[0]
        used[0] += 1
        cp = pltpu.make_async_remote_copy(
            src_ref=src, dst_ref=dst, send_sem=send_sem.at[at], recv_sem=recv_sem.at[at],
            device_id=dev, device_id_type=MESH)
        cp.start()
        pending.append(cp)
        if arrives is None:
            return cp
        return pltpu.make_async_remote_copy(
            src_ref=src, dst_ref=arrives, send_sem=send_sem.at[at], recv_sem=recv_sem.at[at],
            device_id=dev, device_id_type=MESH)

    steps = voxels // KB
    def w_copy(i):
        at = pl.ds(i * KB, KB)
        return pltpu.make_async_copy(w_hbm.at[:, at, :], wv.at[:, at, :], local_sem.at[i])
    vol_copies = []
    for c in range(chunks):
        at = pl.ds(c * rows, rows)
        cp = pltpu.make_async_copy(vol_hbm.at[at, :], vol.at[at, :], local_sem.at[steps + c])
        cp.start()
        vol_copies.append(cp)
        if c == 0:
            for i in range(steps):
                w_copy(i).start()
    meas_copies = []
    for hi in range(2):
        col = pl.multiple_of(hi * band + s * LANES, LANES)
        cp = pltpu.make_async_copy(meas_hbm.at[:, :, pl.ds(col, LANES)], meas.at[hi],
                                   local_sem.at[steps + chunks + hi])
        cp.start()
        meas_copies.append(cp)

    barrier = pltpu.get_barrier_semaphore()
    for k in range(1, 8):
        pl.semaphore_signal(barrier, inc=1, device_id=slab_dev(lax.rem(s + k, 8)), device_id_type=MESH)
    pl.semaphore_signal(barrier, inc=1, device_id=dev_core, device_id_type=MESH)
    for dev in (dev_x, dev_y(1), dev_y(2), dev_y(3)):
        pl.semaphore_signal(barrier, inc=1, device_id=dev, device_id_type=MESH)

    column = lax.broadcasted_iota(jnp.int32, (8, LANES), 1) + s * LANES
    column = column.astype(jnp.float32)

    out_copies = []
    gathered = [[], []]

    def chain(c):
        at_rows = pl.ds(c * rows, rows)
        ext = 8 if c == 0 else 0
        m = rows + 2 * ext
        r = rows + ext
        rr = pl.ds(0, r)
        only = pl.ds(0, rows)
        for t in range(subsets):
            view_t = order_ref[t]
            off = off_ref[view_t]
            shift = jnp.where(off >= band, 0, off)
            if t == 0:
                vol_copies[c].wait()

            def forward(i, carry):
                at = pl.ds(pl.multiple_of(i * KB, KB), KB)
                if t == 0:
                    xk = vol[at_rows, at]
                else:
                    xk = jnp.concatenate(
                        [x1[c, i * (KB // LANES) + j] for j in range(KB // LANES)], axis=1)
                xk = xk.astype(jnp.bfloat16)
                if ext:
                    xk = jnp.concatenate([xk, jnp.ones((2 * ext, KB), jnp.bfloat16)], axis=0)
                if t == 0 and c == 0:
                    w_copy(i).wait()
                    wk = jnp.where(view_t == 0, wv[0, at, :], wv[1, at, :])
                else:
                    wk = wv[view_t, at, :]
                acc[c, pl.ds(0, m), :] += jnp.dot(xk, wk, preferred_element_type=jnp.float32)
                return carry

            acc[c, pl.ds(0, m), :] = jnp.zeros((m, band), jnp.float32)
            if t == 0:
                lax.fori_loop(0, steps, forward, 0)
            else:

                def joined(i, carry):
                    return forward(lax.rem(core + i // 2, 2) * 2 + lax.rem(1 + i, 2), carry)

                lax.fori_loop(0, 1, joined, 0)
                pass_on_rest()
                lax.fori_loop(1, 2, joined, 0)
                yield
                core_in[0].wait_recv()
                core_in[1].wait_recv()
                lax.fori_loop(2, 3, joined, 0)
                core_in[2].wait_recv()
                lax.fori_loop(3, 4, joined, 0)
            folded = pltpu.roll(acc[c, rr, :], shift, 1)
            if ext:
                tail = folded[rows:, :]
                kind = lax.broadcasted_iota(jnp.int32, tail.shape, 0)
                tail = jnp.where(kind < 4, tail, off.astype(jnp.float32))
            for b in range(nb):
                fs[t, c, b, only, :] = folded[:rows, b * LANES:(b + 1) * LANES]
                if ext:
                    fs[t, c, b, pl.ds(rows, ext), :] = tail[:, b * LANES:(b + 1) * LANES]
            if t == 0 and c == 0:
                pl.semaphore_wait(barrier, 12)
            arrivals = []
            for k, (dz, dx) in enumerate(SLAB_PEERS, 1):
                peer = across(dz, dx)
                arrivals.append(remote(fs.at[t, c, peer, rr], fr.at[t, c, k, rr], slab_dev(peer)))
            yield
            fr[t, c, 0, rr, :] = fs[t, c, s, rr, :]
            for cp in arrivals:
                cp.wait_recv()
            if t == 0 and c == 0:
                for cp in meas_copies:
                    cp.wait()
            low = jnp.zeros((rows, LANES), jnp.float32)
            high = jnp.zeros((rows, LANES), jnp.float32)
            masks = []
            for k in range(8):
                offs = fr[t, 0, k, pl.ds(rows + 4, 1), :]
                masks.append(column[0:1, :] >= offs)
            if ext:
                rlow = jnp.zeros((1, LANES), jnp.float32)
                rhigh = jnp.zeros((1, LANES), jnp.float32)
                for k in range(8):
                    part = fr[t, c, k, pl.ds(rows, 1), :]
                    rlow += jnp.where(masks[k], part, 0.0)
                    rhigh += jnp.where(masks[k], 0.0, part)
                rsum[t, 0] = jnp.broadcast_to(jnp.maximum(rlow, 1.0), (8, LANES))
                rsum[t, 1] = jnp.broadcast_to(jnp.maximum(rhigh, 1.0), (8, LANES))
            for k in range(8):
                part = fr[t, c, k, only, :]
                low += jnp.where(masks[k], part, 0.0)
                high += jnp.where(masks[k], 0.0, part)
            seen_low = meas[0, view_t, at_rows, :].astype(jnp.float32)
            seen_high = meas[1, view_t, at_rows, :].astype(jnp.float32)
            low = (seen_low - low) / rsum[t, 0, pl.ds(0, 1), :]
            high = (seen_high - high) / rsum[t, 1, pl.ds(0, 1), :]
            cor[t, 0, at_rows, :] = low
            cor[t, 1, at_rows, :] = high
            arrivals = []
            for k, (dz, dx) in enumerate(SLAB_PEERS, 1):
                gs[t, c, k] = jnp.where(masks[k], low, high)
                arrivals.append(remote(
                    gs.at[t, c, k], gr.at[t, c, s], slab_dev(across(4 - dz, dx)),
                    gr.at[t, c, across(dz, dx)]))
            gr[t, c, s] = jnp.where(masks[0], low, high)
            yield
            for cp in arrivals:
                cp.wait_recv()
            if c == chunks - 1:
                def cols(slab):
                    at = pl.ds(pl.multiple_of(slab * LANES, LANES), LANES)
                    return mis.at[t, :, :, at]
                at = pl.ds(pl.multiple_of(s * LANES, LANES), LANES)
                for hi in range(2):
                    mis[t, hi, :, at] = cor[t, hi]
                for k in (1, 2, 3):
                    far = lax.rem(z + 4 - k, 4) * 2 + xl
                    gathered[t].append((remote(cor.at[t], cols(s), dev_z[k], cols(far))))
            g = jnp.concatenate([gr[t, c, b] for b in range(nb)], axis=1)
            g = pltpu.roll(g, jnp.where(shift == 0, 0, band - shift), 1).astype(jnp.bfloat16)
            bandb[c, only, :] = g
            if ext:
                bandb[c, pl.ds(rows, 2 * ext), :] = jnp.ones((2 * ext, band), jnp.bfloat16)

            def backward(base):
                def step(n, carry):
                    vb = base + n * (KB // LANES)
                    wk = wv[view_t, pl.ds(pl.multiple_of(vb * LANES, LANES), KB), :]
                    res = lax.dot_general(bandb[c, pl.ds(0, m), :], wk, (((1,), (1,)), ((), ())),
                                          preferred_element_type=jnp.float32)
                    for j in range(KB // LANES):
                        bk[t, c, vb + j, rr, :] = res[:r, j * LANES:(j + 1) * LANES]
                    return carry
                lax.fori_loop(0, half * LANES // KB, step, 0, unroll=True)

            theirs = (1 - core) * half
            mine = core * half
            backward(theirs)
            core_in = remote(bk.at[t, c, pl.ds(theirs, half), rr], rc.at[t, c, :, rr], dev_core)
            yield
            backward(mine)
            yield
            core_in.wait_recv()

            def add(block, *others):
                total = bk[t, c, mine + block, rr, :]
                for other in others:
                    total += other[...]
                bk[t, c, mine + block, rr, :] = total

            def theirs_of(block):
                return rc.at[t, c, block, rr]

            other_x = 8 + (1 - xh) * 4
            own_x = 8 + xh * 4
            ins_y, ins_x = [], []
            for j in range(4):
                add(other_x + j, theirs_of(other_x + j))
            ins_x.append(remote(bk.at[t, c, pl.ds(mine + other_x, 4), rr], rx1.at[t, c, :, rr], dev_x))
            for k in (2, 1, 3):
                block = turned(k) * 2
                for j in range(2):
                    add(block + j, theirs_of(block + j))
                ins_y.append(remote(bk.at[t, c, pl.ds(mine + block, 2), rr],
                                    ry0.at[t, c, k - 1, :, rr], dev_y(k)))
            yield
            for cp in ins_x:
                cp.wait_recv()
            last_x, last_y = [], []
            for k in (2, 1, 3, 0):
                block = own_x + turned(k)
                add(block, theirs_of(block), rx1.at[t, c, turned(k), rr])
                if k:
                    last_y.append(remote(bk.at[t, c, mine + block, rr], ry1.at[t, c, k - 1, rr], dev_y(k)))
            for cp in ins_y:
                cp.wait_recv()
            for far in (1, 0):
                at = 1 - xh if far else xh
                block = y * 2 + at
                add(block, theirs_of(block), *[ry0.at[t, c, k, at, rr] for k in range(3)])
                if far:
                    last_x.append(remote(bk.at[t, c, mine + block, rr], rx0.at[t, c, rr], dev_x))
            if c == chunks - 1:
                mate_in = remote(cor.at[t], cols(s), dev_mate, cols(s_mate))
            yield
            x_new = x1 if t == 0 else xo

            def renew(block, j, *others):
                vb = mine + block
                total = bk[t, c, vb, rr, :]
                for other in others:
                    total += other[...]
                if ext:
                    csum[t, j] = total[rows:, :]
                if t == 0:
                    old = vol[at_rows, pl.ds(pl.multiple_of(vb * LANES, LANES), LANES)]
                else:
                    old = x1[c, vb]
                x_new[c, vb] = old + RELAXATION * total[:rows, :] / csum[t, j, pl.ds(0, 1), :]

            def send(at, dev, arrives):
                return remote(at, at, dev, arrives)

            def span(block, count, x_new=x_new):
                return x_new.at[c, pl.ds(mine + block, count)]

            for cp in last_y:
                cp.wait_recv()
            renew(own_x + y, 1, *[ry1.at[t, c, k, rr] for k in range(3)])
            ins_y = [send(span(own_x + y, 1), dev_y(k), span(own_x + turned(4 - k), 1)) for k in (2, 1, 3)]
            for cp in last_x:
                cp.wait_recv()
            renew(y * 2 + xh, 0, rx0.at[t, c, rr])
            ins_x = [send(span(y * 2 + xh, 1), dev_x, span(y * 2 + 1 - xh, 1))]
            if c == chunks - 1:
                mate_in.wait_recv()
                for k in (1, 2, 3):
                    far = lax.rem(z + 4 - k, 4) * 2 + 1 - xl
                    gathered[t].append((remote(cols(s_mate), cols(s_mate), dev_z[k], cols(far))))
            yield
            for cp in ins_y:
                cp.wait_recv()
            last_x = [send(span(own_x, 4), dev_x, span(other_x, 4))]
            for cp in ins_x:
                cp.wait_recv()
            last_y = [send(span(y * 2, 2), dev_y(k), span(turned(4 - k) * 2, 2)) for k in (2, 1, 3)]

            def pass_on(block, count, x_new=x_new):
                return send(x_new.at[c, pl.ds(mine + block, count)], dev_core,
                            x_new.at[c, pl.ds(theirs + block, count)])

            core_in = [pass_on(own_x, 4)]
            yield
            for cp in last_x:
                cp.wait_recv()
            core_in.append(pass_on(other_x, 4))

            def pass_on_rest(last_y=last_y, core_in=core_in, pass_on=pass_on):
                for cp in last_y:
                    cp.wait_recv()
                core_in.append(pass_on(0, 8))

        def lay_out(base):
            for j in range(half // 2):
                at = pl.ds(pl.multiple_of((base + j) * LANES, LANES), LANES)
                obuf[at_rows, at] = xo[c, base + j]

        lay_out(mine + 8)
        pass_on_rest()
        lay_out(mine)
        yield
        core_in[0].wait_recv()
        core_in[1].wait_recv()
        lay_out(theirs + 8)
        core_in[2].wait_recv()
        lay_out(theirs)

    live = [chain(c) for c in range(chunks)]
    marks, drained = [], 0
    for at, c in enumerate(ORDER):
        next(live[c], None)
        marks.append(len(pending))
        if at >= 4 and at < len(ORDER) - 2:
            for cp in pending[drained:marks[at - 4]]:
                cp.wait_send()
            drained = max(drained, marks[at - 4])
        if at == len(ORDER) * 3 // 4:
            for cp in gathered[0]:
                cp.wait_recv()
    for t in range(subsets):
        for cp in gathered[t] if t else ():
            cp.wait_recv()
    for cp in out_copies:
        cp.wait()
    for cp in pending[drained:]:
        cp.wait_send()


def per_device(volume, measured, weights, offsets, order):
    subsets, voxels, band = weights.shape
    slices = volume.shape[0]
    cols = measured.shape[2]
    chunks = CHUNKS
    rows = slices // chunks
    r = rows + 8
    nb = band // LANES
    vb = voxels // LANES
    f32 = jnp.float32
    copies = 34 * subsets * chunks + 7 * subsets
    hbm = pl.BlockSpec(memory_space=pltpu.HBM)
    smem = pl.BlockSpec(memory_space=pltpu.SMEM)
    upd, mis = pl.pallas_call(
        lambda *refs: kernel(chunks, *refs),
        out_shape=(pltpu.VMEM((slices, voxels), f32),
                   pltpu.VMEM((subsets, 2, slices, band), f32)),
        in_specs=[smem, smem, hbm, hbm, hbm],
        out_specs=(pl.BlockSpec(memory_space=pltpu.VMEM), pl.BlockSpec(memory_space=pltpu.VMEM)),
        scratch_shapes=[
            pltpu.VMEM((subsets, voxels, band), jnp.bfloat16),
            pltpu.VMEM((slices, voxels), f32),
            pltpu.VMEM((2, subsets, slices, LANES), jnp.bfloat16),
            pltpu.VMEM((chunks, rows + 16, band), f32),
            pltpu.VMEM((chunks, rows + 16, band), jnp.bfloat16),
            pltpu.VMEM((chunks, vb, rows, LANES), f32),
            pltpu.VMEM((chunks, vb, rows, LANES), f32),
            pltpu.VMEM((subsets, chunks, nb, r, LANES), f32),
            pltpu.VMEM((subsets, chunks, nb, r, LANES), f32),
            pltpu.VMEM((subsets, chunks, nb, rows, LANES), f32),
            pltpu.VMEM((subsets, chunks, nb, rows, LANES), f32),
            pltpu.VMEM((subsets, 2, slices, LANES), f32),
            pltpu.VMEM((subsets, 2, 8, LANES), f32),
            pltpu.VMEM((subsets, 2, 8, LANES), f32),
            pltpu.VMEM((subsets, chunks, vb, r, LANES), f32),
            pltpu.VMEM((subsets, chunks, vb // 2, r, LANES), f32),
            pltpu.VMEM((subsets, chunks, 3, 2, r, LANES), f32),
            pltpu.VMEM((subsets, chunks, r, LANES), f32),
            pltpu.VMEM((subsets, chunks, 3, r, LANES), f32),
            pltpu.VMEM((subsets, chunks, 4, r, LANES), f32),
            pltpu.SemaphoreType.DMA((voxels // KB + chunks * 2 + 2 + subsets,)),
            pltpu.SemaphoreType.DMA((copies,)),
            pltpu.SemaphoreType.DMA((copies,)),
        ],
        compiler_params=pltpu.CompilerParams(
            collective_id=0, has_side_effects=True, vmem_limit_bytes=56 * 2**20),
        name="sart",
    )(order, offsets.reshape(subsets), volume, measured, weights)
    return place(order, upd, mis)


def place_kernel(order_ref, upd, mis, out_upd, out_mis, sem):
    band = mis.shape[3]
    rows = upd.shape[0] // 4
    stores = []
    for t in range(mis.shape[0]):
        view = order_ref[t]
        for hi in range(2):
            stores.append(pltpu.make_async_copy(
                mis.at[t, hi], out_mis.at[view, :, pl.ds(hi * band, band)], sem.at[len(stores)]))
    for i in range(4):
        at = pl.ds(i * rows, rows)
        stores.append(pltpu.make_async_copy(upd.at[at, :], out_upd.at[at, :], sem.at[len(stores)]))
    for cp in stores:
        cp.start()
    for cp in stores:
        cp.wait()


def place(order, upd, mis):
    subsets, _, slices, band = mis.shape
    any_spec = pl.BlockSpec(memory_space=pl.ANY)
    return pl.pallas_call(
        place_kernel,
        out_shape=(jax.ShapeDtypeStruct(upd.shape, upd.dtype),
                   jax.ShapeDtypeStruct((subsets, slices, 2 * band), mis.dtype)),
        in_specs=[pl.BlockSpec(memory_space=pltpu.SMEM), pl.BlockSpec(memory_space=pltpu.VMEM), pl.BlockSpec(memory_space=pltpu.VMEM)],
        out_specs=(any_spec, any_spec),
        scratch_shapes=[pltpu.SemaphoreType.DMA((8,))],
        compiler_params=pltpu.CompilerParams(vmem_limit_bytes=2**20),
        name="place",
    )(order, pltpu.with_memory_space_constraint(upd, pltpu.VMEM),
      pltpu.with_memory_space_constraint(mis, pltpu.VMEM))


def solution(mesh):
    placed = (
        P(None, "slab"),
        P("view", None, None),
        P("view", "slab", None),
        P("view", "slab"),
        P("view"),
    )
    return jax.shard_map(
        per_device,
        mesh=mesh,
        in_specs=placed,
        out_specs=(P(None, "slab"), P("view", None, None)),
        check_vma=False,
    )
```

```python
import jax
import jax.numpy as jnp
from jax import lax
from jax.experimental import pallas as pl
from jax.experimental.pallas import tpu as pltpu
from jax.sharding import PartitionSpec as P

RELAXATION = 0.9
MESH = pl.DeviceIdType.MESH
CHUNKS = 2
LANES = 128
KB = 1024
SLAB_PEERS = ((2, 1), (1, 1), (3, 1), (2, 0), (1, 0), (3, 0), (0, 1))
ORDER = (0, 1) + (0, 1, 0, 1, 0, 0, 1, 1, 0, 1, 0, 1, 0, 1, 0, 0, 1, 1) * 2


def kernel(chunks, order_ref, off_ref, vol_hbm, meas_hbm, w_hbm, obuf, mis,
           wv, vol, meas, acc, bandb, x1, xo, fs, fr, gs, gr, cor, rsum, csum,
           bk, rc, ry0, rx0, ry1, rx1, local_sem, send_sem, recv_sem):
    slices, voxels = vol.shape
    rows = slices // chunks
    band = wv.shape[2]
    subsets = 2
    half = voxels // 2 // LANES
    nb = band // LANES

    s = lax.axis_index("slab")
    v = lax.axis_index("view")
    core = lax.rem(v, 2)
    xh = lax.rem(v // 2, 2)
    y = v // 4
    xl = lax.rem(s, 2)
    z = s // 2

    def slab_dev(other):
        return {"slab": other, "view": v}

    def view_dev(other):
        return {"slab": s, "view": other}

    dev_core = view_dev(v + 1 - 2 * core)

    dev_x = view_dev(v + 2 - 4 * xh)

    def turned(dy):
        return lax.rem(y + dy, 4)

    def dev_y(dy):
        return view_dev(v + 4 * (turned(dy) - y))

    s_mate = s + 1 - 2 * xl
    dev_mate = slab_dev(s_mate)

    def across(dz, dx):
        return lax.rem(z + dz, 4) * 2 + (1 - xl if dx else xl)

    dev_z = [None] + [slab_dev(lax.rem(z + k, 4) * 2 + xl) for k in (1, 2, 3)]

    used = [0]
    pending = []

    def remote(src, dst, dev, arrives=None):
        at = used[0]
        used[0] += 1
        cp = pltpu.make_async_remote_copy(
            src_ref=src, dst_ref=dst, send_sem=send_sem.at[at], recv_sem=recv_sem.at[at],
            device_id=dev, device_id_type=MESH)
        cp.start()
        pending.append(cp)
        if arrives is None:
            return cp
        return pltpu.make_async_remote_copy(
            src_ref=src, dst_ref=arrives, send_sem=send_sem.at[at], recv_sem=recv_sem.at[at],
            device_id=dev, device_id_type=MESH)

    steps = voxels // KB
    def w_copy(i):
        at = pl.ds(i * KB, KB)
        return pltpu.make_async_copy(w_hbm.at[:, at, :], wv.at[:, at, :], local_sem.at[i])
    vol_copies = []
    for c in range(chunks):
        at = pl.ds(c * rows, rows)
        cp = pltpu.make_async_copy(vol_hbm.at[at, :], vol.at[at, :], local_sem.at[steps + c])
        cp.start()
        vol_copies.append(cp)
        if c == 0:
            for i in range(steps):
                w_copy(i).start()
    meas_copies = []
    for hi in range(2):
        col = pl.multiple_of(hi * band + s * LANES, LANES)
        cp = pltpu.make_async_copy(meas_hbm.at[:, :, pl.ds(col, LANES)], meas.at[hi],
                                   local_sem.at[steps + chunks + hi])
        cp.start()
        meas_copies.append(cp)

    barrier = pltpu.get_barrier_semaphore()
    for k in range(1, 8):
        pl.semaphore_signal(barrier, inc=1, device_id=slab_dev(lax.rem(s + k, 8)), device_id_type=MESH)
    pl.semaphore_signal(barrier, inc=1, device_id=dev_core, device_id_type=MESH)
    for dev in (dev_x, dev_y(1), dev_y(2), dev_y(3)):
        pl.semaphore_signal(barrier, inc=1, device_id=dev, device_id_type=MESH)

    column = lax.broadcasted_iota(jnp.int32, (8, LANES), 1) + s * LANES
    column = column.astype(jnp.float32)

    out_copies = []
    gathered = [[], []]

    def chain(c):
        at_rows = pl.ds(c * rows, rows)
        ext = 8 if c == 0 else 0
        m = rows + 2 * ext
        r = rows + ext
        rr = pl.ds(0, r)
        only = pl.ds(0, rows)
        for t in range(subsets):
            view_t = order_ref[t]
            off = off_ref[view_t]
            shift = jnp.where(off >= band, 0, off)
            if t == 0:
                vol_copies[c].wait()

            def forward(i, carry):
                at = pl.ds(pl.multiple_of(i * KB, KB), KB)
                if t == 0:
                    xk = vol[at_rows, at]
                else:
                    xk = jnp.concatenate(
                        [x1[c, i * (KB // LANES) + j] for j in range(KB // LANES)], axis=1)
                xk = xk.astype(jnp.bfloat16)
                if ext:
                    xk = jnp.concatenate([xk, jnp.ones((2 * ext, KB), jnp.bfloat16)], axis=0)
                if t == 0 and c == 0:
                    w_copy(i).wait()
                    wk = jnp.where(view_t == 0, wv[0, at, :], wv[1, at, :])
                else:
                    wk = wv[view_t, at, :]
                acc[c, pl.ds(0, m), :] += jnp.dot(xk, wk, preferred_element_type=jnp.float32)
                return carry

            acc[c, pl.ds(0, m), :] = jnp.zeros((m, band), jnp.float32)
            if t == 0:
                lax.fori_loop(0, steps, forward, 0)
            else:

                def joined(i, carry):
                    return forward(lax.rem(core + i // 2, 2) * 2 + lax.rem(1 + i, 2), carry)

                lax.fori_loop(0, 1, joined, 0)
                pass_on_rest()
                lax.fori_loop(1, 2, joined, 0)
                yield
                core_in[0].wait_recv()
                core_in[1].wait_recv()
                lax.fori_loop(2, 3, joined, 0)
                core_in[2].wait_recv()
                lax.fori_loop(3, 4, joined, 0)
            folded = pltpu.roll(acc[c, rr, :], shift, 1)
            if ext:
                tail = folded[rows:, :]
                kind = lax.broadcasted_iota(jnp.int32, tail.shape, 0)
                tail = jnp.where(kind < 4, tail, off.astype(jnp.float32))
            for b in range(nb):
                fs[t, c, b, only, :] = folded[:rows, b * LANES:(b + 1) * LANES]
                if ext:
                    fs[t, c, b, pl.ds(rows, ext), :] = tail[:, b * LANES:(b + 1) * LANES]
            if t == 0 and c == 0:
                pl.semaphore_wait(barrier, 12)
            arrivals = []
            for k, (dz, dx) in enumerate(SLAB_PEERS, 1):
                peer = across(dz, dx)
                arrivals.append(remote(fs.at[t, c, peer, rr], fr.at[t, c, k, rr], slab_dev(peer)))
            yield
            fr[t, c, 0, rr, :] = fs[t, c, s, rr, :]
            for cp in arrivals:
                cp.wait_recv()
            if t == 0 and c == 0:
                for cp in meas_copies:
                    cp.wait()
            low = jnp.zeros((rows, LANES), jnp.float32)
            high = jnp.zeros((rows, LANES), jnp.float32)
            masks = []
            for k in range(8):
                offs = fr[t, 0, k, pl.ds(rows + 4, 1), :]
                masks.append(column[0:1, :] >= offs)
            if ext:
                rlow = jnp.zeros((1, LANES), jnp.float32)
                rhigh = jnp.zeros((1, LANES), jnp.float32)
                for k in range(8):
                    part = fr[t, c, k, pl.ds(rows, 1), :]
                    rlow += jnp.where(masks[k], part, 0.0)
                    rhigh += jnp.where(masks[k], 0.0, part)
                rsum[t, 0] = jnp.broadcast_to(jnp.maximum(rlow, 1.0), (8, LANES))
                rsum[t, 1] = jnp.broadcast_to(jnp.maximum(rhigh, 1.0), (8, LANES))
            for k in range(8):
                part = fr[t, c, k, only, :]
                low += jnp.where(masks[k], part, 0.0)
                high += jnp.where(masks[k], 0.0, part)
            seen_low = meas[0, view_t, at_rows, :].astype(jnp.float32)
            seen_high = meas[1, view_t, at_rows, :].astype(jnp.float32)
            low = (seen_low - low) / rsum[t, 0, pl.ds(0, 1), :]
            high = (seen_high - high) / rsum[t, 1, pl.ds(0, 1), :]
            cor[t, 0, at_rows, :] = low
            cor[t, 1, at_rows, :] = high
            arrivals = []
            for k, (dz, dx) in enumerate(SLAB_PEERS, 1):
                gs[t, c, k] = jnp.where(masks[k], low, high)
                arrivals.append(remote(
                    gs.at[t, c, k], gr.at[t, c, s], slab_dev(across(4 - dz, dx)),
                    gr.at[t, c, across(dz, dx)]))
            gr[t, c, s] = jnp.where(masks[0], low, high)
            yield
            for cp in arrivals:
                cp.wait_recv()
            g = jnp.concatenate([gr[t, c, b] for b in range(nb)], axis=1)
            g = pltpu.roll(g, jnp.where(shift == 0, 0, band - shift), 1).astype(jnp.bfloat16)
            bandb[c, only, :] = g
            if ext:
                bandb[c, pl.ds(rows, 2 * ext), :] = jnp.ones((2 * ext, band), jnp.bfloat16)

            def backward(base):
                def step(n, carry):
                    vb = base + n * (KB // LANES)
                    wk = wv[view_t, pl.ds(pl.multiple_of(vb * LANES, LANES), KB), :]
                    res = lax.dot_general(bandb[c, pl.ds(0, m), :], wk, (((1,), (1,)), ((), ())),
                                          preferred_element_type=jnp.float32)
                    for j in range(KB // LANES):
                        bk[t, c, vb + j, rr, :] = res[:r, j * LANES:(j + 1) * LANES]
                    return carry
                lax.fori_loop(0, half * LANES // KB, step, 0, unroll=True)

            theirs = (1 - core) * half
            mine = core * half
            backward(theirs)
            core_in = remote(bk.at[t, c, pl.ds(theirs, half), rr], rc.at[t, c, :, rr], dev_core)
            if c == chunks - 1:
                def cols(slab):
                    at = pl.ds(pl.multiple_of(slab * LANES, LANES), LANES)
                    return mis.at[t, :, :, at]
                at = pl.ds(pl.multiple_of(s * LANES, LANES), LANES)
                for hi in range(2):
                    mis[t, hi, :, at] = cor[t, hi]
                for k in (1, 2, 3):
                    far = lax.rem(z + 4 - k, 4) * 2 + xl
                    gathered[t].append((remote(cor.at[t], cols(s), dev_z[k], cols(far))))
            yield
            backward(mine)
            yield
            core_in.wait_recv()

            def add(block, *others):
                total = bk[t, c, mine + block, rr, :]
                for other in others:
                    total += other[...]
                bk[t, c, mine + block, rr, :] = total

            def theirs_of(block):
                return rc.at[t, c, block, rr]

            other_x = 8 + (1 - xh) * 4
            own_x = 8 + xh * 4
            ins_y, ins_x = [], []
            for k in (2, 1, 3):
                block = turned(k) * 2
                for j in range(2):
                    add(block + j, theirs_of(block + j))
                ins_y.append(remote(bk.at[t, c, pl.ds(mine + block, 2), rr],
                                    ry0.at[t, c, k - 1, :, rr], dev_y(k)))
            for j in range(4):
                add(other_x + j, theirs_of(other_x + j))
            ins_x.append(remote(bk.at[t, c, pl.ds(mine + other_x, 4), rr], rx1.at[t, c, :, rr], dev_x))
            yield
            for cp in ins_x:
                cp.wait_recv()
            last_x, last_y = [], []
            for k in (2, 1, 3, 0):
                block = own_x + turned(k)
                add(block, theirs_of(block), rx1.at[t, c, turned(k), rr])
                if k:
                    last_y.append(remote(bk.at[t, c, mine + block, rr], ry1.at[t, c, k - 1, rr], dev_y(k)))
            for cp in ins_y:
                cp.wait_recv()
            for far in (1, 0):
                at = 1 - xh if far else xh
                block = y * 2 + at
                add(block, theirs_of(block), *[ry0.at[t, c, k, at, rr] for k in range(3)])
                if far:
                    last_x.append(remote(bk.at[t, c, mine + block, rr], rx0.at[t, c, rr], dev_x))
            if c == chunks - 1:
                mate_in = remote(cor.at[t], cols(s), dev_mate, cols(s_mate))
            yield
            x_new = x1 if t == 0 else xo

            def renew(block, j, *others):
                vb = mine + block
                total = bk[t, c, vb, rr, :]
                for other in others:
                    total += other[...]
                if ext:
                    csum[t, j] = total[rows:, :]
                if t == 0:
                    old = vol[at_rows, pl.ds(pl.multiple_of(vb * LANES, LANES), LANES)]
                else:
                    old = x1[c, vb]
                x_new[c, vb] = old + RELAXATION * total[:rows, :] / csum[t, j, pl.ds(0, 1), :]

            def send(at, dev, arrives):
                return remote(at, at, dev, arrives)

            def span(block, count, x_new=x_new):
                return x_new.at[c, pl.ds(mine + block, count)]

            for cp in last_y:
                cp.wait_recv()
            renew(own_x + y, 1, *[ry1.at[t, c, k, rr] for k in range(3)])
            ins_y = [send(span(own_x + y, 1), dev_y(k), span(own_x + turned(4 - k), 1)) for k in (2, 1, 3)]
            for cp in last_x:
                cp.wait_recv()
            renew(y * 2 + xh, 0, rx0.at[t, c, rr])
            ins_x = [send(span(y * 2 + xh, 1), dev_x, span(y * 2 + 1 - xh, 1))]
            if c == chunks - 1:
                mate_in.wait_recv()
                for k in (1, 2, 3):
                    far = lax.rem(z + 4 - k, 4) * 2 + 1 - xl
                    gathered[t].append((remote(cols(s_mate), cols(s_mate), dev_z[k], cols(far))))
            yield
            for cp in ins_y:
                cp.wait_recv()
            last_x = [send(span(own_x, 4), dev_x, span(other_x, 4))]
            for cp in ins_x:
                cp.wait_recv()
            last_y = [send(span(y * 2, 2), dev_y(k), span(turned(4 - k) * 2, 2)) for k in (2, 1, 3)]

            def pass_on(block, count, x_new=x_new):
                return send(x_new.at[c, pl.ds(mine + block, count)], dev_core,
                            x_new.at[c, pl.ds(theirs + block, count)])

            core_in = [pass_on(own_x, 4)]
            yield
            for cp in last_x:
                cp.wait_recv()
            core_in.append(pass_on(other_x, 4))

            def pass_on_rest(last_y=last_y, core_in=core_in, pass_on=pass_on):
                for cp in last_y:
                    cp.wait_recv()
                core_in.append(pass_on(0, 8))

        def lay_out(base):
            for j in range(half // 2):
                at = pl.ds(pl.multiple_of((base + j) * LANES, LANES), LANES)
                obuf[at_rows, at] = xo[c, base + j]

        lay_out(mine + 8)
        pass_on_rest()
        lay_out(mine)
        yield
        core_in[0].wait_recv()
        core_in[1].wait_recv()
        lay_out(theirs + 8)
        core_in[2].wait_recv()
        lay_out(theirs)

    live = [chain(c) for c in range(chunks)]
    marks, drained = [], 0
    for at, c in enumerate(ORDER):
        next(live[c], None)
        marks.append(len(pending))
        if at >= 4 and at < len(ORDER) - 2:
            for cp in pending[drained:marks[at - 4]]:
                cp.wait_send()
            drained = max(drained, marks[at - 4])
        if at == len(ORDER) * 3 // 4:
            for cp in gathered[0]:
                cp.wait_recv()
    for t in range(subsets):
        for cp in gathered[t] if t else ():
            cp.wait_recv()
    for cp in out_copies:
        cp.wait()
    for cp in pending[drained:]:
        cp.wait_send()


def per_device(volume, measured, weights, offsets, order):
    subsets, voxels, band = weights.shape
    slices = volume.shape[0]
    cols = measured.shape[2]
    chunks = CHUNKS
    rows = slices // chunks
    r = rows + 8
    nb = band // LANES
    vb = voxels // LANES
    f32 = jnp.float32
    copies = 34 * subsets * chunks + 7 * subsets
    hbm = pl.BlockSpec(memory_space=pltpu.HBM)
    smem = pl.BlockSpec(memory_space=pltpu.SMEM)
    upd, mis = pl.pallas_call(
        lambda *refs: kernel(chunks, *refs),
        out_shape=(pltpu.VMEM((slices, voxels), f32),
                   pltpu.VMEM((subsets, 2, slices, band), f32)),
        in_specs=[smem, smem, hbm, hbm, hbm],
        out_specs=(pl.BlockSpec(memory_space=pltpu.VMEM), pl.BlockSpec(memory_space=pltpu.VMEM)),
        scratch_shapes=[
            pltpu.VMEM((subsets, voxels, band), jnp.bfloat16),
            pltpu.VMEM((slices, voxels), f32),
            pltpu.VMEM((2, subsets, slices, LANES), jnp.bfloat16),
            pltpu.VMEM((chunks, rows + 16, band), f32),
            pltpu.VMEM((chunks, rows + 16, band), jnp.bfloat16),
            pltpu.VMEM((chunks, vb, rows, LANES), f32),
            pltpu.VMEM((chunks, vb, rows, LANES), f32),
            pltpu.VMEM((subsets, chunks, nb, r, LANES), f32),
            pltpu.VMEM((subsets, chunks, nb, r, LANES), f32),
            pltpu.VMEM((subsets, chunks, nb, rows, LANES), f32),
            pltpu.VMEM((subsets, chunks, nb, rows, LANES), f32),
            pltpu.VMEM((subsets, 2, slices, LANES), f32),
            pltpu.VMEM((subsets, 2, 8, LANES), f32),
            pltpu.VMEM((subsets, 2, 8, LANES), f32),
            pltpu.VMEM((subsets, chunks, vb, r, LANES), f32),
            pltpu.VMEM((subsets, chunks, vb // 2, r, LANES), f32),
            pltpu.VMEM((subsets, chunks, 3, 2, r, LANES), f32),
            pltpu.VMEM((subsets, chunks, r, LANES), f32),
            pltpu.VMEM((subsets, chunks, 3, r, LANES), f32),
            pltpu.VMEM((subsets, chunks, 4, r, LANES), f32),
            pltpu.SemaphoreType.DMA((voxels // KB + chunks * 2 + 2 + subsets,)),
            pltpu.SemaphoreType.DMA((copies,)),
            pltpu.SemaphoreType.DMA((copies,)),
        ],
        compiler_params=pltpu.CompilerParams(
            collective_id=0, has_side_effects=True, vmem_limit_bytes=56 * 2**20),
        name="sart",
    )(order, offsets.reshape(subsets), volume, measured, weights)
    return place(order, upd, mis)


def place_kernel(order_ref, upd, mis, out_upd, out_mis, sem):
    band = mis.shape[3]
    rows = upd.shape[0] // 4
    stores = []
    for t in range(mis.shape[0]):
        view = order_ref[t]
        for hi in range(2):
            stores.append(pltpu.make_async_copy(
                mis.at[t, hi], out_mis.at[view, :, pl.ds(hi * band, band)], sem.at[len(stores)]))
    for i in range(4):
        at = pl.ds(i * rows, rows)
        stores.append(pltpu.make_async_copy(upd.at[at, :], out_upd.at[at, :], sem.at[len(stores)]))
    for cp in stores:
        cp.start()
    for cp in stores:
        cp.wait()


def place(order, upd, mis):
    subsets, _, slices, band = mis.shape
    any_spec = pl.BlockSpec(memory_space=pl.ANY)
    return pl.pallas_call(
        place_kernel,
        out_shape=(jax.ShapeDtypeStruct(upd.shape, upd.dtype),
                   jax.ShapeDtypeStruct((subsets, slices, 2 * band), mis.dtype)),
        in_specs=[pl.BlockSpec(memory_space=pltpu.SMEM), pl.BlockSpec(memory_space=pltpu.VMEM), pl.BlockSpec(memory_space=pltpu.VMEM)],
        out_specs=(any_spec, any_spec),
        scratch_shapes=[pltpu.SemaphoreType.DMA((8,))],
        compiler_params=pltpu.CompilerParams(vmem_limit_bytes=2**20),
        name="place",
    )(order, pltpu.with_memory_space_constraint(upd, pltpu.VMEM),
      pltpu.with_memory_space_constraint(mis, pltpu.VMEM))


def solution(mesh):
    placed = (
        P(None, "slab"),
        P("view", None, None),
        P("view", "slab", None),
        P("view", "slab"),
        P("view"),
    )
    return jax.shard_map(
        per_device,
        mesh=mesh,
        in_specs=placed,
        out_specs=(P(None, "slab"), P("view", None, None)),
        check_vma=False,
    )
```
